512 devices in a mesh: edge: 32 (over x, z), feat: 16 (over y, core).
Axes of the slice: x: 4, y: 8, z: 8, core: 2. Of those that a mesh axis runs over, the one named last changes fastest.
Arguments:
- features: bfloat16 [16384, 2048], P('edge', 'feat'), may hold values from -6 to 6
- tiles: bfloat16 [1536, 128, 128], P('edge'), may hold values from -0.0546875 to 0.0546875
- tile_slot: int32 [12288], P('edge'), may hold values from 0 to 127, as said below
- tile_col: int32 [12288], P('edge'), may hold values from 0 to 3, as said below
- tile_id: int32 [12288], P('edge'), may hold values from 0 to 47
- touched: int32 [32, 32, 4], replicated, may hold values from 0 to 3, as said below
- weight: bfloat16 [2048, 2048], P(None, 'feat'), may hold values from -0.125 to 0.125
- readers: int32 [512], P('edge'), may hold values from 0 to 127, as said below
Outputs:
- hidden: bfloat16 [16384, 2048], P('edge', 'feat')
- ghosts: bfloat16 [65536, 2048], P('edge', 'feat')
The draws below stay inside these ranges and needn't reach their ends.
Inputs may be any that keep to these rules, and one draw needn't show every extreme that they name: For each sender and owner, the 4 entries of touched are distinct block numbers below 4. Within one device's 384 listed products, the pairs (tile_slot, tile_col) are all distinct. Within one device's 384 listed products, the pairs (tile_slot, tile_col) are all distinct. `readers`: one device's 16 entries are distinct, and at most 2 of them lie in the row blocks of any one index of edge; every device's list has some index of edge with exactly 2.
All inputs are finite; a program needn't handle non-finite values.
Results may differ from the reference program's by a relative error of at most 0.0049.
Values may be sent and summed in bfloat16 or wider, within the bound.
A program may use at most 128 MiB of HBM per device.

```python
import math
import jax
import jax.numpy as jnp
from jax import lax

F = 2048
BLOCK = 128
TABLE = 48
CAP = 4
READ = 16
RCAP = 2
BLK_DEV = 4
TILES = 384
VERTS = 16384
NBLOCKS = 128
N_EDGE = 32


def draw_touched(key, part):
    scores = jax.random.randint(key, (N_EDGE, N_EDGE, BLK_DEV), 0, 1 << 20) * BLK_DEV
    scores = scores + jnp.arange(BLK_DEV, dtype=jnp.int32)
    order = jnp.argsort(scores, axis=-1)
    return order[:, :, :CAP].astype(jnp.int32)


def listed_pairs(key):
    base = jax.random.fold_in(key, 11)
    slot_total = N_EDGE * CAP
    offsets = jax.random.randint(jax.random.fold_in(base, 1), (N_EDGE,), 0, BLK_DEV)
    slot_list = jnp.repeat(jnp.arange(slot_total, dtype=jnp.int32), BLK_DEV - 1)
    stepping = jnp.tile(jnp.arange(BLK_DEV - 1, dtype=jnp.int32), slot_total)
    columns = (slot_list[None, :] + offsets[:, None] + 1 + stepping[None, :]) % BLK_DEV
    slot_rows = jnp.broadcast_to(slot_list[None, :], (N_EDGE, TILES))
    device_keys = jax.random.split(jax.random.fold_in(base, 2), N_EDGE)
    order = jax.vmap(lambda k: jax.random.permutation(k, TILES))(device_keys)
    slot_out = jnp.take_along_axis(slot_rows, order, axis=1)
    column_out = jnp.take_along_axis(columns, order, axis=1)
    return (slot_out.reshape(-1).astype(jnp.int32), column_out.reshape(-1).astype(jnp.int32))


def draw_tile_slot(key, part):
    return listed_pairs(key)[0]


def draw_tile_col(key, part):
    return listed_pairs(key)[1]


def draw_readers(key, part):
    base = jax.random.fold_in(key, 23)
    slot_total = N_EDGE * RCAP

    def one_list(device_key):
        first_key, owner_key, block_key, shuffle_key = jax.random.split(device_key, 4)
        scores = jax.random.randint(first_key, (slot_total,), 0, 1 << 20) * slot_total + jnp.arange(slot_total, dtype=jnp.int32)
        first_owner = jax.random.randint(owner_key, (), 0, N_EDGE)
        owner_of = jnp.arange(slot_total, dtype=jnp.int32) // RCAP
        scores = jnp.where(owner_of == first_owner, jnp.arange(slot_total, dtype=jnp.int32) - slot_total, scores)
        picked = jnp.argsort(scores)[:READ].astype(jnp.int32)
        owners = picked // RCAP
        within = picked % RCAP
        block_scores = jax.random.randint(block_key, (N_EDGE, BLK_DEV), 0, 1 << 20) * BLK_DEV + jnp.arange(BLK_DEV, dtype=jnp.int32)
        block_order = jnp.argsort(block_scores, axis=-1).astype(jnp.int32)
        chosen = owners * BLK_DEV + block_order[owners, within]
        return chosen[jax.random.permutation(shuffle_key, READ)]
    device_keys = jax.random.split(base, N_EDGE)
    return jax.vmap(one_list)(device_keys).reshape(-1).astype(jnp.int32)


def with_ends(result, rng, low, top_value):
    spot = [jax.random.randint(jax.random.fold_in(rng, axis), (), 0, length) for axis, length in enumerate(result.shape)]
    widest = result.shape.index(max(result.shape))
    neighbour = spot[:widest] + [(spot[widest] + 1) % result.shape[widest]] + spot[widest + 1:]
    return result.at[tuple(spot)].set(low).at[tuple(neighbour)].set(top_value)


def shard_levels(stream_key, dims, cuts, low, top_value):
    level, own = 1.0, jax.random.fold_in(stream_key, 6)
    for axis_at, parts in cuts:
        steps = jnp.exp(jax.random.uniform(jax.random.fold_in(own, axis_at), (parts,), jnp.float32, low / len(cuts), top_value / len(cuts)))
        level = level * jnp.repeat(steps, dims[axis_at] // parts).reshape([-1 if axis == axis_at else 1 for axis in range(len(dims))])
    return level


def scatter_about(rng, shape, width, reach, pieces=(), kind=jnp.bfloat16):
    entries = width * jax.random.normal(rng, shape, jnp.float32)
    if pieces:
        entries = entries * shard_levels(rng, shape, pieces, -0.22, 0.18)
    return jnp.clip(entries, -reach, reach).astype(kind)


def setup_inputs(seed: int = 0) -> dict:
    key_list = jax.random.split(jax.random.key(seed), 9)
    return {
        "features": scatter_about(key_list[0], (VERTS, F), 1.0, 6.0, ((0, 32), (1, 16))),
        "tiles": scatter_about(key_list[1], (N_EDGE * TABLE, BLOCK, BLOCK), (BLOCK * TILES // BLK_DEV) ** -0.5, 0.0546875, ((0, 32),)),
        "tile_slot": draw_tile_slot(jax.random.fold_in(key_list[8], 71), 0),
        "tile_col": draw_tile_col(jax.random.fold_in(key_list[8], 71), 0),
        "tile_id": with_ends(jax.random.randint(key_list[4], (N_EDGE * TILES,), 0, TABLE), jax.random.fold_in(key_list[4], 1), 0, TABLE - 1).astype(jnp.int32),
        "touched": draw_touched(jax.random.fold_in(key_list[8], 71), 0),
        "weight": scatter_about(key_list[6], (F, F), F ** -0.5, 0.125, ((1, 16),)),
        "readers": draw_readers(jax.random.fold_in(key_list[8], 71), 0),
    }


def reference(features, tiles, tile_slot, tile_col, tile_id, touched, weight, readers):
    per_step = math.gcd(TILES, 64)
    everyone = N_EDGE * TILES
    blocked = features.reshape(NBLOCKS, BLOCK, F)

    def add_group(turn, running):
        first_pos = (turn * per_step).astype(jnp.int32)
        positions = first_pos + jnp.arange(per_step, dtype=jnp.int32)
        device = positions // TILES
        slots = lax.dynamic_slice_in_dim(tile_slot, first_pos, per_step)
        columns = lax.dynamic_slice_in_dim(tile_col, first_pos, per_step)
        chosen = lax.dynamic_slice_in_dim(tile_id, first_pos, per_step)
        owner = slots // CAP
        local_block = touched[device, owner, slots % CAP]
        target = owner * BLK_DEV + local_block
        source = device * BLK_DEV + columns
        adjacency = tiles[device * TABLE + chosen].astype(jnp.float32)
        inputs = blocked[source].astype(jnp.float32)
        product = jnp.einsum("gij,gjc->gic", adjacency, inputs, precision=lax.Precision.HIGHEST)
        return running.at[target].add(product)

    summed = lax.fori_loop(0, everyone // per_step, add_group, jnp.zeros((NBLOCKS, BLOCK, F), jnp.float32))
    aggregated = summed.reshape(VERTS, F).astype(jnp.bfloat16)
    hidden = jnp.maximum(jnp.dot(aggregated, weight, preferred_element_type=jnp.float32), 0.0).astype(jnp.bfloat16)
    ghosts = hidden.reshape(NBLOCKS, BLOCK, F)[readers].reshape(N_EDGE * READ * BLOCK, F)
    return hidden, ghosts
```

```python
import functools

import jax
import jax.numpy as jnp
import numpy as np
from jax import lax
from jax.experimental import pallas as pl
from jax.experimental.pallas import tpu as pltpu
from jax.sharding import PartitionSpec as P

NX, NZ, NY, NC = 4, 8, 8, 2
HOP_US = 1.5
LINK = 46.5e3
MESH_ID = pl.DeviceIdType.MESH
SIGNS = (1, -1)


def offsets(n):
    h = n // 2
    out = [h] if n > 1 else []
    for r in range(h - 1, 0, -1):
        out += [r, n - r]
    return out + [0]


def halves_of(sign, r, n):
    lead = 0 if sign > 0 else 1
    return [lead] if r == n // 2 else [1 - lead, lead]


class Plan:
    def __init__(self):
        self.steps = {}
        self.units = {}

    def unit(self, name, link, blocks, src, dst):
        self.units[name] = dict(link=link, blocks=blocks, src=src, dst=dst, index=len(self.units))

    def step(self, name, fn=None, after=(), recv=(), send=(), cost=0.02):
        self.steps[name] = dict(fn=fn, after=list(after), recv=[r for r in recv if r in self.units or True], send=list(send), cost=cost)

    def order(self, block_bytes):
        sender = {u: s for s, v in self.steps.items() for u in v["send"]}
        needed = {s: [] for s in self.steps}
        for s, v in self.steps.items():
            for a in v["after"]:
                needed[a].append((s, 0.0))
            for u in v["recv"]:
                wire = self.units[u]["blocks"] * block_bytes / LINK
                needed[sender[u]].append((s, wire + HOP_US))
        path = {}

        def length(s):
            if s not in path:
                path[s] = self.steps[s]["cost"] + max([d + length(t) for t, d in needed[s]] + [0.0])
            return path[s]

        for s in self.steps:
            length(s)
        core, links, arrival, done, left, result = 0.0, {}, {}, {}, set(self.steps), []
        names = list(self.steps)
        while left:
            best = None
            for s in names:
                v = self.steps[s]
                if s not in left or any(a not in done for a in v["after"]) or any(u not in arrival for u in v["recv"]):
                    continue
                ready = max([done[a] for a in v["after"]] + [arrival[u] for u in v["recv"]] + [core])
                key = (ready, -path[s])
                if best is None or key < best[0]:
                    best = (key, s)
            (ready, _), s = best
            left.remove(s)
            result.append(s)
            core = ready + self.steps[s]["cost"]
            done[s] = core
            for u in self.steps[s]["send"]:
                link = self.units[u]["link"]
                rate = LINK if link[0] != "core" else 8 * LINK
                begin = max(core, links.get(link, 0.0))
                links[link] = begin + self.units[u]["blocks"] * block_bytes / rate
                arrival[u] = links[link] + HOP_US
        self.total = core
        return result


def need_order():
    zu = {s: [(r, half) for r in range(NZ // 2, 0, -1) for half in halves_of(s, r, NZ)] for s in SIGNS}
    subs = 2 if NZ >= 4 else 1
    xu = {s: [] for s in SIGNS}
    for s in SIGNS:
        for r in range(NX // 2, 0, -1):
            for sub in range(subs):
                xu[s] += [(r, half, sub) for half in halves_of(s, r, NX)]
    zoff, xoff = offsets(NZ), offsets(NX)
    width = NZ // subs
    blocks, where, seg = [], {}, []
    slots = max(len(zu[1]), len(xu[1]))
    for t in range(slots):
        begin = len(blocks)
        for s in SIGNS:
            if t < len(zu[s]):
                r, half = zu[s][t]
                where["z", s, r, half] = (len(blocks), t)
                blocks += [(rx, s * r % NZ, half) for rx in xoff]
        for s in SIGNS:
            if t < len(xu[s]):
                r, half, sub = xu[s][t]
                where["x", s, r, half, sub] = (len(blocks), t)
                blocks += [(s * r % NX, rz, 2 + half) for rz in zoff[sub * width:(sub + 1) * width]]
        seg.append((begin, len(blocks)))
    begin = len(blocks)
    for sub in range(subs):
        for half in (0, 1):
            where["x", 0, half, sub] = (len(blocks), slots)
            blocks += [(0, rz, 2 + half) for rz in zoff[sub * width:(sub + 1) * width]]
    for half in (0, 1):
        where["z", 0, half] = (len(blocks), slots)
        blocks += [(rx, 0, half) for rx in xoff]
    seg.append((begin, len(blocks)))
    return zu, xu, subs, blocks, where, seg


def kernel(plan_only, table, picks, features, tiles, weight, hidden, ghosts, *scratch):
    (bank, mix, part, zs, zr, xs, xr, z2s, z2r, x2s, x2r, qz, qx, gy, g, send_sem, recv_sem, local_sem) = scratch
    zu, xu, subs, blocks, where, seg = need_order()
    plan = Plan()
    hx, hz, hy = NX // 2, NZ // 2, NY // 2
    zoff, xoff = offsets(NZ), offsets(NX)
    width = NZ // subs
    size = features.shape[1]
    rows = features.shape[0] // 4
    deep = tiles.shape[0]
    if not plan_only:
        edge, feat = lax.axis_index("edge"), lax.axis_index("feat")
        x, z, y, core = edge // NZ, edge % NZ, feat // NC, feat % NC
        peers = {}
        for s in SIGNS:
            peers["x", s] = (((x + s + NX) % NX) * NZ + z, feat)
            peers["z", s] = (x * NZ + (z + s + NZ) % NZ, feat)
            peers["y", s] = (edge, ((y + s + NY) % NY) * NC + core)
        peers["core", 1] = (edge, y * NC + (core + 1) % NC)
        greeted = [k for k, n in ((("x", 1), NX), (("x", -1), NX), (("z", 1), NZ), (("z", -1), NZ), (("y", 1), NY), (("y", -1), NY), (("core", 1), NC)) if n > 1]
        loads = [pltpu.make_async_copy(tiles, bank.at[pl.ds(0, deep)], local_sem.at[0])]
        for ry in range(NY):
            for rc in range(NC):
                row = ((y + ry) % NY * NC + (core + rc) % NC) * size
                loads.append(
                    pltpu.make_async_copy(
                        weight.at[pl.ds(pl.multiple_of(row, size), size)],
                        mix.at[pl.ds((ry * NC + rc) * size, size)],
                        local_sem.at[1 + ry * NC + rc],
                    )
                )
        for c in loads:
            c.start()
        barrier = pltpu.get_barrier_semaphore()
        for k in greeted:
            pl.semaphore_signal(barrier, inc=1, device_id=peers[k], device_id_type=MESH_ID)
        bank[deep] = jnp.zeros_like(bank[deep])
        loads[0].wait()

    def products(lo, hi):
        def body(i, carry):
            wide = jnp.concatenate([bank[table[i * 4 + c]] for c in range(4)], axis=1)
            part[i] = jnp.dot(wide, features[...], preferred_element_type=jnp.float32)
            return carry

        lax.fori_loop(lo, hi, body, 0)

    def total(count, own, extra, put):
        def body(k, carry):
            value = own(k)
            for e in extra:
                value = value + e(k).astype(jnp.float32)
            put(k, value)
            return carry

        lax.fori_loop(0, count, body, 0) if count > 1 else body(0, 0)

    for t, (lo, hi) in enumerate(seg):
        plan.step(("P", t), functools.partial(products, lo, hi), cost=0.05 * (hi - lo), after=[("P", t - 1)] if t else [])

    def exists(sign, r, half, n):
        return 1 <= r <= n // 2 and half in halves_of(sign, r, n)

    def store(ref, *lead):
        def put(k, value):
            ref[(*lead, k)] = value.astype(ref.dtype)

        return put

    def put_one(ref, *lead):
        def put(k, value):
            ref[lead] = value.astype(ref.dtype)

        return put

    zi = {s: {u: i for i, u in enumerate(zu[s])} for s in SIGNS}
    for s in SIGNS:
        d = 0 if s > 0 else 1
        for (r, half), i in zi[s].items():
            plan.unit(("Z1", s, r, half), ("z", s), NX, (zs, (d, i)), (zr, (d, i)))
    for s in SIGNS:
        d = 0 if s > 0 else 1
        for (r, half), i in zi[s].items():
            base, t = where["z", s, r, half]
            back = exists(s, r + 1, half, NZ)
            extra = [functools.partial(lambda d, j, k: zr[d, j, k], d, zi[s][r + 1, half])] if back else []
            plan.step(
                ("Z1", s, r, half),
                functools.partial(total, NX, functools.partial(lambda b, k: part[b + k], base), extra, store(zs, d, i)),
                after=[("P", t)], recv=[("Z1", s, r + 1, half)] if back else [], send=[("Z1", s, r, half)], cost=0.15,
            )
    for half in (0, 1):
        base, t = where["z", 0, half]
        near = [s for s in SIGNS if exists(s, 1, half, NZ)]
        plan.step(
            ("Z1f", half),
            functools.partial(total, NX, functools.partial(lambda b, k: part[b + k], base),
                              [functools.partial(lambda d, j, k: zr[d, j, k], 0 if s > 0 else 1, zi[s][1, half]) for s in near], store(qz, half)),
            after=[("P", t)], recv=[("Z1", s, 1, half) for s in near], cost=0.15,
        )

    xi = {s: {u: i for i, u in enumerate(xu[s])} for s in SIGNS}
    for s in SIGNS:
        d = 0 if s > 0 else 1
        for (r, half, sub), i in xi[s].items():
            plan.unit(("X1", s, r, half, sub), ("x", s), width, (xs, (d, i)), (xr, (d, i)))
    for s in SIGNS:
        d = 0 if s > 0 else 1
        for (r, half, sub), i in xi[s].items():
            base, t = where["x", s, r, half, sub]
            back = exists(s, r + 1, half, NX)
            extra = [functools.partial(lambda d, j, k: xr[d, j, k], d, xi[s][r + 1, half, sub])] if back else []
            plan.step(
                ("X1", s, r, half, sub),
                functools.partial(total, width, functools.partial(lambda b, k: part[b + k], base), extra, store(xs, d, i)),
                after=[("P", t)], recv=[("X1", s, r + 1, half, sub)] if back else [], send=[("X1", s, r, half, sub)], cost=0.15,
            )
    for sub in range(subs):
        for half in (0, 1):
            base, t = where["x", 0, half, sub]
            near = [s for s in SIGNS if exists(s, 1, half, NX)]

            def put(k, value, half=half, sub=sub):
                qx[half, sub * width + k] = value

            plan.step(
                ("X1f", half, sub),
                functools.partial(total, width, functools.partial(lambda b, k: part[b + k], base),
                                  [functools.partial(lambda d, j, k: xr[d, j, k], 0 if s > 0 else 1, xi[s][1, half, sub]) for s in near], put),
                after=[("P", t)], recv=[("X1", s, 1, half, sub) for s in near], cost=0.15,
            )

    for tag, axis, n, off, q, sref, rref, first in (
        ("Z2", "x", NX, xoff, qz, z2s, z2r, lambda half, p: [("Z1f", half)]),
        ("X2", "z", NZ, zoff, qx, x2s, x2r, lambda half, p: [("X1f", half, p // width)]),
    ):
        units = {s: [(r, half) for r in range(n // 2, 0, -1) for half in halves_of(s, r, n)] for s in SIGNS}
        for s in SIGNS:
            d = 0 if s > 0 else 1
            for i, (r, half) in enumerate(units[s]):
                plan.unit((tag, s, r, half), (axis, s), 1, (sref, (d, i)), (rref, (d, i)))
        for s in SIGNS:
            d = 0 if s > 0 else 1
            for i, (r, half) in enumerate(units[s]):
                p = off.index(s * r % n)
                back = exists(s, r + 1, half, n)
                extra = []
                if back:
                    extra = [functools.partial(lambda ref, d, j, k: ref[d, j], rref, d, units[s].index((r + 1, half)))]
                plan.step(
                    (tag, s, r, half),
                    functools.partial(total, 1, functools.partial(lambda q, half, p, k: q[half, p], q, half, p), extra, put_one(sref, d, i)),
                    after=first(half, p), recv=[(tag, s, r + 1, half)] if back else [], send=[(tag, s, r, half)], cost=0.05,
                )
        for half in (0, 1):
            near = [s for s in SIGNS if exists(s, 1, half, n)]
            p = off.index(0)
            plan.step(
                (tag + "f", half),
                functools.partial(total, 1, functools.partial(lambda q, half, p, k: q[half, p], q, half, p),
                                  [functools.partial(lambda ref, d, j, k: ref[d, j], rref, 0 if s > 0 else 1, units[s].index((1, half))) for s in near],
                                  put_one(gy, 0 if tag == "Z2" else 1, 0, 0, half)),
                after=first(half, p), recv=[(tag, s, 1, half) for s in near], cost=0.05,
            )

    for f in (0, 1):
        ready = [(("Z2f", "X2f")[f], half) for half in (0, 1)]
        arrivals = []

        def part_of(sign, d, n):
            if d + 1 < n // 2:
                return 0, 2
            return (0 if sign > 0 else 1), 1

        if NC > 1:
            plan.unit(("YP", f, 0), ("core", 1), 2, (gy, (f, 0, 0)), (gy, (f, 0, 1)))
            arrivals.append(("YP", f, 0))
        for s in SIGNS:
            for d in range(hy):
                a, c = part_of(s, d, NY)
                here, there = -s * d % NY, -s * (d + 1) % NY
                plan.unit(("Y", f, s, d), ("y", s), c, (gy, (f, here, 0, pl.ds(a, c))), (gy, (f, there, 0, pl.ds(a, c))))
                arrivals.append(("Y", f, s, d))
                if NC > 1:
                    plan.unit(("YP", f, s, d + 1), ("core", 1), c, (gy, (f, there, 0, pl.ds(a, c))), (gy, (f, there, 1, pl.ds(a, c))))
                    arrivals.append(("YP", f, s, d + 1))
        send = ([("Y", f, s, 0) for s in SIGNS] if NY > 1 else []) + ([("YP", f, 0)] if NC > 1 else [])
        plan.step(("Yown", f), after=ready, send=send)
        for s in SIGNS:
            for d in range(1, hy + 1):
                send = ([("Y", f, s, d)] if d < hy else []) + ([("YP", f, s, d)] if NC > 1 else [])
                plan.step(("Yfwd", f, s, d), recv=[("Y", f, s, d - 1)], send=send)

        def mixing(f=f):
            for half in (0, 1):
                wide = jnp.concatenate([gy[f, ry, rc, half] for ry in range(NY) for rc in range(NC)], axis=1)
                value = jnp.maximum(jnp.dot(wide, mix[...], preferred_element_type=jnp.float32), 0.0).astype(jnp.bfloat16)
                g[f * NX * NZ * 2 + half] = value
                hidden[pl.ds((2 * f + half) * rows, rows)] = value

        plan.step(("H", f), mixing, after=[("W",), ("Yown", f)], recv=arrivals, cost=1.0)

    def weights():
        for c in loads[1:]:
            c.wait()

    plan.step(("W",), weights, after=[("P", len(seg) - 1)])

    everything = []
    for f in (0, 1):
        (a1, n1), (a2, n2) = ((("x", NX), ("z", NZ)), (("z", NZ), ("x", NX)))[f]

        def slot(q1, q2, a=0, f=f, n2=n2):
            return f * NX * NZ * 2 + (q1 * n2 + q2) * 2 + a

        def gref(q1, q2, a, c, slot=slot):
            return (g, (pl.ds(slot(q1, q2, a), c),))

        for s in SIGNS:
            for d in range(n1 // 2):
                a, c = part_of(s, d, n1)
                plan.unit(("E1", f, s, d), (a1, s), c, gref(-s * d % n1, 0, a, c), gref(-s * (d + 1) % n1, 0, a, c))
                everything.append(("E1", f, s, d))
        for q in range(n1):
            for s in SIGNS:
                for d in range(n2 // 2):
                    a, c = part_of(s, d, n2)
                    plan.unit(("E2", f, q, s, d), (a2, s), c, gref(q, -s * d % n2, a, c), gref(q, -s * (d + 1) % n2, a, c))
                    everything.append(("E2", f, q, s, d))
        plan.step(("Eown", f), after=[("H", f)], send=[("E1", f, s, 0) for s in SIGNS] + [("E2", f, 0, s, 0) for s in SIGNS])
        for d in range(1, n1 // 2 + 1):
            for s in SIGNS:
                if d < n1 // 2:
                    q = -s * d % n1
                    plan.step(("E1f", f, s, d), recv=[("E1", f, s, d - 1)], send=[("E1", f, s, d)] + [("E2", f, q, t, 0) for t in SIGNS])
            if d == n1 // 2:
                plan.step(("E1f", f, 0, d), recv=[("E1", f, s, d - 1) for s in SIGNS], send=[("E2", f, d, t, 0) for t in SIGNS])
        for q in range(n1):
            for s in SIGNS:
                for d in range(1, n2 // 2):
                    plan.step(("E2f", f, q, s, d), recv=[("E2", f, q, s, d - 1)], send=[("E2", f, q, s, d)])

    def gather():
        def body(r, carry):
            ghosts[pl.ds(pl.multiple_of(r * rows, rows), rows)] = g[picks[r]]
            return carry

        lax.fori_loop(0, picks.shape[0], body, 0)

    plan.step(("G",), gather, after=[("H", 0), ("H", 1)], recv=everything, cost=1.0)

    order = plan.order(rows * size * 2)
    if plan_only:
        return plan, order

    def copy(name):
        u = plan.units[name]
        (sref, sat), (dref, dat) = u["src"], u["dst"]
        return pltpu.make_async_remote_copy(
            src_ref=sref.at[sat], dst_ref=dref.at[dat], send_sem=send_sem.at[u["index"]], recv_sem=recv_sem.at[u["index"]],
            device_id=peers[u["link"]], device_id_type=MESH_ID,
        )

    copies = {name: copy(name) for name in plan.units}
    arrived, opened = set(), False
    for name in order:
        step = plan.steps[name]
        for u in step["recv"]:
            if u not in arrived:
                copies[u].wait_recv()
                arrived.add(u)
        if step["fn"] is not None:
            step["fn"]()
        if step["send"] and not opened:
            pl.semaphore_wait(barrier, len(greeted))
            opened = True
        for u in step["send"]:
            copies[u].start()
    for name in plan.units:
        if name not in arrived:
            copies[name].wait_recv()
        copies[name].wait_send()


def scratch_shapes(rows, size, deep):
    zu, xu, subs, blocks, where, seg = need_order()
    width = NZ // subs
    bf, fp = jnp.bfloat16, jnp.float32

    def units(n):
        return len([1 for r in range(n // 2, 0, -1) for half in halves_of(1, r, n)])

    v = pltpu.VMEM
    shapes = [
        v((deep + 1, rows, rows), bf), v((NY * NC * size, size), bf), v((len(blocks), rows, size), fp),
        v((2, len(zu[1]), NX, rows, size), bf), v((2, len(zu[1]), NX, rows, size), bf),
        v((2, len(xu[1]), width, rows, size), bf), v((2, len(xu[1]), width, rows, size), bf),
        v((2, units(NX), rows, size), bf), v((2, units(NX), rows, size), bf),
        v((2, units(NZ), rows, size), bf), v((2, units(NZ), rows, size), bf),
        v((2, NX, rows, size), fp), v((2, NZ, rows, size), fp),
        v((2, NY, NC, 2, rows, size), bf), v((4 * NX * NZ, rows, size), bf),
    ]
    return shapes


def local(features, tiles, tile_slot, tile_col, tile_id, touched, weight, readers):
    edge = lax.axis_index("edge")
    x, z = edge // NZ, edge % NZ
    block = tiles.shape[1]
    size = features.shape[1]
    deep = tiles.shape[0]
    cap = touched.shape[2]
    zu, xu, subs, blocks, where, seg = need_order()
    at = np.array(blocks, np.int32)
    owner = (x + at[:, 0]) % NX * NZ + (z + at[:, 1]) % NZ
    wanted = owner * 4 + at[:, 2]
    mine = lax.dynamic_index_in_dim(touched, edge, 0, keepdims=False).reshape(-1)
    slots = jnp.arange(mine.shape[0], dtype=jnp.int32)
    target_of = slots // cap * 4 + mine
    target = jnp.sum(jnp.where(tile_slot[:, None] == slots[None, :], target_of[None, :], 0), axis=1)
    pair = target * 4 + tile_col
    keys = (wanted[:, None] * 4 + jnp.arange(4, dtype=jnp.int32)[None, :]).reshape(-1)
    table = deep + jnp.sum(jnp.where(keys[:, None] == pair[None, :], tile_id[None, :] - deep, 0), axis=1)
    o, j = readers // 4, readers % 4
    rx, rz = (o // NZ - x + NX) % NX, (o % NZ - z + NZ) % NZ
    picks = jnp.where(j < 2, (rx * NZ + rz) * 2 + j, NX * NZ * 2 + (rz * NX + rx) * 2 + j - 2)
    plan, order = kernel(True, table, picks, features, tiles, weight, None, None, *([None] * 18))
    count = len(plan.units)
    vmem = pl.BlockSpec(memory_space=pltpu.VMEM)
    smem = pl.BlockSpec(memory_space=pltpu.SMEM)
    anywhere = pl.BlockSpec(memory_space=pl.ANY)
    hidden, ghosts = pl.pallas_call(
        functools.partial(kernel, False),
        out_shape=(
            jax.ShapeDtypeStruct(features.shape, jnp.bfloat16),
            jax.ShapeDtypeStruct((readers.shape[0] * block, size), jnp.bfloat16),
        ),
        in_specs=[smem, smem, vmem, anywhere, anywhere],
        out_specs=(vmem, vmem),
        scratch_shapes=scratch_shapes(block, size, deep)
        + [pltpu.SemaphoreType.DMA((count,)), pltpu.SemaphoreType.DMA((count,)), pltpu.SemaphoreType.DMA((1 + NY * NC,))],
        compiler_params=pltpu.CompilerParams(collective_id=0, has_side_effects=True, vmem_limit_bytes=52 << 20),
        name="layer",
    )(table.astype(jnp.int32), picks.astype(jnp.int32), features, tiles, weight)
    return hidden, ghosts


def solution(mesh):
    in_specs = (
        P("edge", "feat"),
        P("edge", None, None),
        P("edge"),
        P("edge"),
        P("edge"),
        P(),
        P(None, "feat"),
        P("edge"),
    )
    out_specs = (P("edge", "feat"), P("edge", "feat"))
    return jax.shard_map(local, mesh=mesh, in_specs=in_specs, out_specs=out_specs, check_vma=False)
```

```python
import functools

import jax
import jax.numpy as jnp
import numpy as np
from jax import lax
from jax.experimental import pallas as pl
from jax.experimental.pallas import tpu as pltpu
from jax.sharding import PartitionSpec as P

NX, NZ, NY, NC = 4, 8, 8, 2
STREAMS = ("z", "x", "z", "x")
HOP_US, LINK, GROUP_US, AHEAD_US = 1.9, 46.5e3, 0.3, 1.5
MESH_ID = pl.DeviceIdType.MESH
SIGNS = (1, -1)


def offsets(n):
    h = n // 2
    out = [h] if n > 1 else []
    for r in range(h - 1, 0, -1):
        out += [r, n - r]
    return out + [0]


def groups_of(n):
    h = n // 2
    out, at = [[0]], 1
    for d in range(1, h + 1):
        count = 1 if 2 * d == n else 2
        out.append(list(range(at, at + count)))
        at += count
    return out


def lead(sign):
    return 0 if sign > 0 else 1


def halves_of(sign, r, n):
    if not 1 <= r <= n // 2:
        return []
    return [lead(sign)] if r == n // 2 else [0, 1]


def sizes(kind):
    return (NZ, NX) if kind == "z" else (NX, NZ)


def subs_of(kind):
    second = sizes(kind)[1]
    return second // 4 if second > 4 else 1


class Plan:
    def __init__(self):
        self.steps = {}
        self.units = {}

    def unit(self, name, link, blocks, src, dst):
        self.units[name] = dict(link=link, blocks=blocks, src=src, dst=dst, index=len(self.units))

    def step(self, name, fn=None, after=(), recv=(), send=(), cost=0.02, wave=0):
        self.steps[name] = dict(fn=fn, after=list(after), recv=list(recv), send=list(send), cost=cost, wave=wave)

    def order(self, block_bytes):
        sender = {u: s for s, v in self.steps.items() for u in v["send"]}
        needed = {s: [] for s in self.steps}
        for s, v in self.steps.items():
            for a in v["after"]:
                needed[a].append((s, 0.0))
            for u in v["recv"]:
                needed[sender[u]].append((s, self.units[u]["blocks"] * block_bytes / LINK + HOP_US))
        path = {}

        def length(s):
            if s not in path:
                path[s] = self.steps[s]["cost"] + max([d + length(t) for t, d in needed[s]] + [0.0])
            return path[s]

        for s in self.steps:
            length(s)
        core, links, arrival, done, left, result = 0.0, {}, {}, {}, list(self.steps), []
        while left:
            best = None
            for s in left:
                v = self.steps[s]
                if any(a not in done for a in v["after"]) or any(u not in arrival for u in v["recv"]):
                    continue
                ready = max([done[a] for a in v["after"]] + [arrival[u] for u in v["recv"]] + [core])
                begin = max([ready] + [links.get(self.units[u]["link"], 0.0) - AHEAD_US for u in v["send"]])
                key = (round(begin / 0.2), v["wave"], -path[s])
                if best is None or key < best[0]:
                    best = (key, s, ready)
            _, s, ready = best
            left.remove(s)
            result.append(s)
            core = ready + self.steps[s]["cost"]
            done[s] = core
            for u in self.steps[s]["send"]:
                link = self.units[u]["link"]
                rate = LINK if link[0] != "core" else 8 * LINK
                begin = max(core, links.get(link, 0.0))
                links[link] = begin + self.units[u]["blocks"] * block_bytes / rate
                arrival[u] = links[link] + HOP_US
        self.total = core
        return result


def need_order():
    blocks, where, seg = [], {}, []
    for wave in range(len(STREAMS) // 2):
        pair = [2 * wave, 2 * wave + 1]
        rest = {st: [(off, sub) for off in offsets(sizes(STREAMS[st])[0]) for sub in range(subs_of(STREAMS[st]))] for st in pair}
        if NX > 1:
            for st in pair:
                n = sizes(STREAMS[st])[0]
                rank = {o: min(o, n - o) for o in range(n)}
                rest[st].sort(key=lambda u: (u[0] == 0, (rank[u[0]] != n // 2) * u[1], -rank[u[0]]))
        slots = 5
        for t in range(slots):
            begin = len(blocks)
            for st in pair:
                n, second = sizes(STREAMS[st])
                mine = rest[st]
                take = -(-len(mine) // (slots - t))
                for off, sub in mine[:take]:
                    where[st, off, sub] = (len(blocks), len(seg))
                    far = offsets(second)
                    width = second // subs_of(STREAMS[st])
                    for other in far[sub * width:(sub + 1) * width]:
                        blocks.append(((other, off) if STREAMS[st] == "z" else (off, other)) + (st,))
                rest[st] = mine[take:]
            seg.append((wave, begin, len(blocks)))
    return blocks, where, seg


def kernel(plan_only, group, table, lists, readers, seq, features, tiles, weight, hidden, ghosts, *scratch):
    feats, bank, mix, part, gy, g, send_sem, recv_sem, local_sem = scratch[:9]
    per = [scratch[9 + 5 * st:14 + 5 * st] for st in range(len(STREAMS))]
    blocks, where, seg = need_order()
    plan = Plan()
    size = features.shape[1]
    rows = features.shape[0] // 4
    deep = tiles.shape[0]
    mid = rows // 2
    if not plan_only:
        edge, feat = lax.axis_index("edge"), lax.axis_index("feat")
        x, z, y, core = edge // NZ, edge % NZ, feat // NC, feat % NC
        peers = {}
        for s in SIGNS:
            peers["x", s] = (((x + s + NX) % NX) * NZ + z, feat)
            peers["z", s] = (x * NZ + (z + s + NZ) % NZ, feat)
            peers["y", s] = (edge, ((y + s + NY) % NY) * NC + core)
        peers["core", 1] = (edge, y * NC + (core + 1) % NC)
        greeted = [k for k in peers if {"x": NX, "z": NZ, "y": NY, "core": NC}[k[0]] > 1]
        barrier = pltpu.get_barrier_semaphore()
        for k in greeted:
            pl.semaphore_signal(barrier, inc=1, device_id=peers[k], device_id_type=MESH_ID)
        loads = [
            pltpu.make_async_copy(tiles, bank.at[pl.ds(0, deep)], local_sem.at[0]),
            pltpu.make_async_copy(features, feats, local_sem.at[1]),
        ]
        for ry in range(NY):
            row = (y + ry) % NY * NC * size
            loads.append(
                pltpu.make_async_copy(
                    weight.at[pl.ds(pl.multiple_of(row, size), NC * size)],
                    mix.at[pl.ds(ry * NC * size, NC * size)],
                    local_sem.at[2 + ry],
                )
            )
        for c in loads:
            c.start()
        bank[deep] = jnp.zeros_like(bank[deep])
        loads[0].wait()
        loads[1].wait()

    def products(lo, hi):
        def body(i, carry):
            parts = []
            for b in range(group):
                v = seq[i * group + b]
                j = v % 4
                owner = (x + v // 1024) % NX * NZ + (z + v // 4 % 256) % NZ
                slot = jnp.int32(0)
                for c in range(4):
                    slot = slot + jnp.where(lists[owner * 4 + c] == j, c, 0)
                base = (owner * 4 + slot % 4) * 4
                parts.append(jnp.concatenate([bank[table[base + c]] for c in range(4)], axis=1))
            value = jnp.dot(jnp.concatenate(parts, axis=0), feats[...], preferred_element_type=jnp.float32)
            part[pl.ds(i * group, group)] = value.reshape(group, rows, size)
            return carry

        lax.fori_loop(lo // group, hi // group, body, 0)

    for t, (wave, lo, hi) in enumerate(seg):
        plan.step(("P", t), functools.partial(products, lo, hi), cost=GROUP_US * (hi - lo) / 4, after=[("P", t - 1)] if t else [], wave=wave)

    def cut(half):
        return pl.ds(half * mid, mid)

    def total(count, own, extras, put):
        def body(k, carry):
            for half, more in extras:
                value = own(k, half)
                for e in more:
                    value = value + e(k, half).astype(jnp.float32)
                put(k, half, value)
            return carry

        lax.fori_loop(0, count, body, 0) if count > 1 else body(0, 0)

    everything = []
    for st, kind in enumerate(STREAMS):
        wave = st // 2
        n1, n2 = sizes(kind)
        a1, a2 = ("z", "x") if kind == "z" else ("x", "z")
        h1, h2, hy = n1 // 2, n2 // 2, NY // 2
        subs = subs_of(kind)
        width = n2 // subs
        off2 = offsets(n2)
        s1, r1, s2, r2, q = per[st]

        def unit1(s, r, sub, ref, st=st, width=width, n1=n1):
            hv = halves_of(s, r, n1)
            return ref, (lead(s), r - 1, pl.ds(sub * width, width), pl.ds(hv[0] * mid, mid * len(hv)))

        for s in SIGNS:
            for r in range(1, h1 + 1):
                for sub in range(subs):
                    plan.unit(("A", st, s, r, sub), (a1, s), width * len(halves_of(s, r, n1)) / 2, unit1(s, r, sub, s1), unit1(s, r, sub, r1))

        def in1(s, r, sub, k, half, r1=r1, width=width):
            return r1[lead(s), r - 1, sub * width + k, cut(half)]

        for s in SIGNS:
            for r in range(h1, 0, -1):
                for sub in range(subs):
                    base, t = where[st, s * r % n1, sub]

                    def own(k, half, base=base):
                        return part[base + k, cut(half)]

                    def put(k, half, value, s=s, r=r, sub=sub, s1=s1, width=width):
                        s1[lead(s), r - 1, sub * width + k, cut(half)] = value.astype(jnp.bfloat16)

                    extras = [
                        (half, [functools.partial(in1, s, r + 1, sub)] if half in halves_of(s, r + 1, n1) else [])
                        for half in halves_of(s, r, n1)
                    ]
                    plan.step(
                        ("A", st, s, r, sub), functools.partial(total, width, own, extras, put), after=[("P", t)],
                        recv=[("A", st, s, r + 1, sub)] if r < h1 else [], send=[("A", st, s, r, sub)], cost=0.15, wave=wave,
                    )
        for sub in range(subs):
            base, t = where[st, 0, sub]

            def own(k, half, base=base):
                return part[base + k, cut(half)]

            def put(k, half, value, sub=sub, q=q, width=width):
                q[sub * width + k, cut(half)] = value

            extras = [(half, [functools.partial(in1, s, 1, sub) for s in SIGNS if half in halves_of(s, 1, n1)]) for half in (0, 1)]
            plan.step(
                ("Af", st, sub), functools.partial(total, width, own, extras, put), after=[("P", t)],
                recv=[("A", st, s, 1, sub) for s in SIGNS] if n1 > 1 else [], cost=0.15, wave=wave,
            )

        def unit2(s, r, ref, n2=n2):
            hv = halves_of(s, r, n2)
            return ref, (lead(s), r - 1, pl.ds(hv[0] * mid, mid * len(hv)))

        for s in SIGNS:
            for r in range(1, h2 + 1):
                plan.unit(("B", st, s, r), (a2, s), len(halves_of(s, r, n2)) / 2, unit2(s, r, s2), unit2(s, r, r2))

        def in2(s, r, k, half, r2=r2):
            return r2[lead(s), r - 1, cut(half)]

        for s in SIGNS:
            for r in range(h2, 0, -1):
                p = off2.index(s * r % n2)

                def own(k, half, p=p, q=q):
                    return q[p, cut(half)]

                def put(k, half, value, s=s, r=r, s2=s2):
                    s2[lead(s), r - 1, cut(half)] = value.astype(jnp.bfloat16)

                extras = [
                    (half, [functools.partial(in2, s, r + 1)] if half in halves_of(s, r + 1, n2) else []) for half in halves_of(s, r, n2)
                ]
                plan.step(
                    ("B", st, s, r), functools.partial(total, 1, own, extras, put), after=[("Af", st, p // width)],
                    recv=[("B", st, s, r + 1)] if r < h2 else [], send=[("B", st, s, r)], cost=0.06, wave=wave,
                )
        p = off2.index(0)

        def own(k, half, p=p, q=q):
            return q[p, cut(half)]

        def put(k, half, value, st=st):
            gy[st, 0, 0, cut(half)] = value.astype(jnp.bfloat16)

        extras = [(half, [functools.partial(in2, s, 1) for s in SIGNS if half in halves_of(s, 1, n2)]) for half in (0, 1)]
        plan.step(
            ("Bf", st), functools.partial(total, 1, own, extras, put), after=[("Af", st, p // width)],
            recv=[("B", st, s, 1) for s in SIGNS] if n2 > 1 else [], cost=0.06, wave=wave,
        )

        def rows_of(s, d, n):
            hv = halves_of(s, d + 1, n)
            return pl.ds(hv[0] * mid, mid * len(hv)), len(hv) / 2

        arrivals = []
        if NC > 1:
            plan.unit(("YP", st, 0, 0), ("core", 1), 1, (gy, (st, 0, 0)), (gy, (st, 0, 1)))
            arrivals.append(("YP", st, 0, 0))
        for s in SIGNS:
            for d in range(hy):
                w, c = rows_of(s, d, NY)
                here, there = -s * d % NY, -s * (d + 1) % NY
                plan.unit(("Y", st, s, d), ("y", s), c, (gy, (st, here, 0, w)), (gy, (st, there, 0, w)))
                arrivals.append(("Y", st, s, d))
                if NC > 1:
                    plan.unit(("YP", st, s, d + 1), ("core", 1), c, (gy, (st, there, 0, w)), (gy, (st, there, 1, w)))
                    arrivals.append(("YP", st, s, d + 1))
        send = ([("Y", st, s, 0) for s in SIGNS] if NY > 1 else []) + ([("YP", st, 0, 0)] if NC > 1 else [])
        plan.step(("Y", st), after=[("Bf", st)], send=send, wave=wave)
        for s in SIGNS:
            for d in range(1, hy + 1):
                send = ([("Y", st, s, d)] if d < hy else []) + ([("YP", st, s, d)] if NC > 1 else [])
                plan.step(("Y", st, s, d), recv=[("Y", st, s, d - 1)], send=send, wave=wave)

        def slot(qpos, q2, st=st, n1=n1):
            return st * NX * NZ + q2 * n1 + qpos

        def mixing(st=st, slot=slot):
            def wide(swap):
                order = [(ry, (rc + swap) % NC) for ry in range(NY) for rc in range(NC)]
                value = jnp.dot(
                    jnp.concatenate([gy[st, ry, rc] for ry, rc in order], axis=1), mix[...], preferred_element_type=jnp.float32
                )
                value = jnp.maximum(value, 0.0).astype(jnp.bfloat16)
                g[slot(0, 0)] = value
                hidden[pl.ds(st * rows, rows)] = value

            for c in range(NC):
                pl.when(core == c)(functools.partial(wide, c))

        plan.step(("H", st), mixing, after=[("W",), ("Y", st)], recv=arrivals, cost=0.7, wave=wave)

        back1 = offsets(n1)[::-1]
        where1 = {o: i for i, o in enumerate(back1)}
        sets = groups_of(n1)
        for s in SIGNS:
            for d in range(h1):
                w, c = rows_of(s, d, n1)
                plan.unit(
                    ("C", st, s, d), (a1, s), c, (g, (slot(where1[-s * d % n1], 0), w)), (g, (slot(where1[-s * (d + 1) % n1], 0), w))
                )
                everything.append(("C", st, s, d))
        for i, members in enumerate(sets):
            for s in SIGNS:
                for d in range(h2):
                    w, c = rows_of(s, d, n2)
                    here = pl.ds(slot(members[0], -s * d % n2), len(members))
                    there = pl.ds(slot(members[0], -s * (d + 1) % n2), len(members))
                    plan.unit(("D", st, i, s, d), (a2, s), c * len(members), (g, (here, w)), (g, (there, w)))
                    everything.append(("D", st, i, s, d))
        second = lambda i: [("D", st, i, s, 0) for s in SIGNS] if h2 else []
        plan.step(("C", st), after=[("H", st)], send=[("C", st, s, 0) for s in SIGNS] if h1 else [], wave=wave)
        plan.step(("D", st, 0), after=[("H", st)], send=second(0), wave=wave)
        for d in range(1, h1 + 1):
            for s in SIGNS:
                if d < h1:
                    plan.step(("C", st, s, d), recv=[("C", st, s, d - 1)], send=[("C", st, s, d)], wave=wave)
            plan.step(("D", st, d), recv=[("C", st, s, d - 1) for s in SIGNS], send=second(d), wave=wave)
        for i in range(len(sets)):
            for s in SIGNS:
                for d in range(1, h2):
                    plan.step(("D", st, i, s, d), recv=[("D", st, i, s, d - 1)], send=[("D", st, i, s, d)], wave=wave)

    def weights():
        for c in loads[2:]:
            c.wait()

    plan.step(("W",), weights, after=[("P", len(seg) - 1)])

    def place(q, n):
        return jnp.where(2 * q < n, 2 * q, 2 * (n - q) - 1) % n

    def gather():
        def body(r, carry):
            v = readers[r]
            o, j = v // 4, v % 4
            rx, rz = (o // NZ - x + NX) % NX, (o % NZ - z + NZ) % NZ
            at = j * NX * NZ + jnp.where(j % 2 == 0, rx * NZ + place(rz, NZ), rz * NX + place(rx, NX))
            ghosts[pl.ds(pl.multiple_of(r * rows, rows), rows)] = g[at]
            return carry

        lax.fori_loop(0, readers.shape[0], body, 0)

    plan.step(("G",), gather, after=[("H", st) for st in range(len(STREAMS))], recv=everything, cost=0.5, wave=9)

    order = plan.order(rows * size * 2)
    if plan_only:
        return plan, order

    def copy(name):
        u = plan.units[name]
        (sref, sat), (dref, dat) = u["src"], u["dst"]
        return pltpu.make_async_remote_copy(
            src_ref=sref.at[sat], dst_ref=dref.at[dat], send_sem=send_sem.at[u["index"]], recv_sem=recv_sem.at[u["index"]],
            device_id=peers[u["link"]], device_id_type=MESH_ID,
        )

    copies = {name: copy(name) for name in plan.units}
    arrived, opened = set(), False
    for name in order:
        step = plan.steps[name]
        for u in step["recv"]:
            if u not in arrived:
                copies[u].wait_recv()
                arrived.add(u)
        if step["fn"] is not None:
            step["fn"]()
        if step["send"] and not opened:
            pl.semaphore_wait(barrier, len(greeted))
            opened = True
        for u in step["send"]:
            copies[u].start()
    for name in plan.units:
        if name not in arrived:
            copies[name].wait_recv()
        copies[name].wait_send()


def scratch_shapes(rows, size, deep, count):
    bf, fp, v = jnp.bfloat16, jnp.float32, pltpu.VMEM
    blocks, where, seg = need_order()
    shapes = [
        v((4 * rows, size), bf), v((deep + 1, rows, rows), bf), v((NY * NC * size, size), bf), v((len(blocks), rows, size), fp),
        v((len(STREAMS), NY, NC, rows, size), bf), v((len(STREAMS) * NX * NZ, rows, size), bf),
        pltpu.SemaphoreType.DMA((count,)), pltpu.SemaphoreType.DMA((count,)), pltpu.SemaphoreType.DMA((2 + NY,)),
    ]
    for kind in STREAMS:
        n1, n2 = sizes(kind)
        first, second = v((2, max(n1 // 2, 1), n2, rows, size), bf), v((2, max(n2 // 2, 1), rows, size), bf)
        shapes += [first, first, second, second, v((n2, rows, size), fp)]
    return shapes


def local(features, tiles, tile_slot, tile_col, tile_id, touched, weight, readers):
    edge = lax.axis_index("edge")
    block = tiles.shape[1]
    size = features.shape[1]
    deep = tiles.shape[0]
    blocks, where, seg = need_order()
    group = 4 if all((hi - lo) % 4 == 0 for _, lo, hi in seg) else 1
    seq = jnp.array([rx * 1024 + rz * 4 + j for rx, rz, j in blocks], jnp.int32)
    lists = lax.dynamic_index_in_dim(touched, edge, 0, keepdims=False).reshape(-1)
    keys = jnp.arange(lists.shape[0] * 4, dtype=jnp.int32)
    pair = tile_slot * 4 + tile_col
    table = deep + jnp.sum(jnp.where(keys[:, None] == pair[None, :], tile_id[None, :] - deep, 0), axis=1)
    args = (table.astype(jnp.int32), lists, readers, seq, features, tiles, weight)
    plan, order = kernel(True, group, *args, None, None, *([None] * 29))
    vmem = pl.BlockSpec(memory_space=pltpu.VMEM)
    smem = pl.BlockSpec(memory_space=pltpu.SMEM)
    hbm = pl.BlockSpec(memory_space=pltpu.HBM)
    return pl.pallas_call(
        functools.partial(kernel, False, group),
        out_shape=(
            jax.ShapeDtypeStruct(features.shape, jnp.bfloat16),
            jax.ShapeDtypeStruct((readers.shape[0] * block, size), jnp.bfloat16),
        ),
        in_specs=[smem, smem, smem, smem, hbm, hbm, hbm],
        out_specs=(vmem, vmem),
        scratch_shapes=scratch_shapes(block, size, deep, len(plan.units)),
        compiler_params=pltpu.CompilerParams(collective_id=0, has_side_effects=True, vmem_limit_bytes=60 << 20),
        name="layer",
    )(*args)


def solution(mesh):
    in_specs = (
        P("edge", "feat"),
        P("edge", None, None),
        P("edge"),
        P("edge"),
        P("edge"),
        P(),
        P(None, "feat"),
        P("edge"),
    )
    out_specs = (P("edge", "feat"), P("edge", "feat"))
    return jax.shard_map(local, mesh=mesh, in_specs=in_specs, out_specs=out_specs, check_vma=False)
```

```python
import functools

import jax
import jax.numpy as jnp
import numpy as np
from jax import lax
from jax.experimental import pallas as pl
from jax.experimental.pallas import tpu as pltpu
from jax.sharding import PartitionSpec as P

NX, NZ, NY, NC = 4, 8, 8, 2
STREAMS = ("x", "z", "x", "z")
PRE = (False, False, True, True)
WAVES = (0, 0, 1, 1)
FIRST = ('z', 'x', 'z', 'x')
DIRECT = {"B": (), "C": (), "Y": False}
SUBS = {"z": 2, "x": 4}
HOP_US, LINK, GROUP_US, AHEAD_US, FAR_US = 2.3, 46.5e3, 0.3, 0.5, 0.8
LATER_US = (1.5, 0.0)
MESH_ID = pl.DeviceIdType.MESH
SIGNS = (1, -1)


def offsets(n):
    h = n // 2
    out = [h] if n > 1 else []
    for r in range(h - 1, 0, -1):
        out += [r, n - r]
    return out + [0]


def groups_of(n):
    h = n // 2
    out, at = [[0]], 1
    for d in range(1, h + 1):
        count = 1 if 2 * d == n else 2
        out.append(list(range(at, at + count)))
        at += count
    return out


def lead(sign):
    return 0 if sign > 0 else 1


def halves_of(sign, r, n):
    if not 1 <= r <= n // 2:
        return []
    return [lead(sign)] if r == n // 2 else [0, 1]


def sizes(kind):
    return (NZ, NX) if kind == "z" else (NX, NZ)


def subs_of(kind):
    return SUBS[kind] if sizes(kind)[1] >= 4 else 1


class Plan:
    def __init__(self):
        self.steps = {}
        self.units = {}

    def unit(self, name, link, blocks, src, dst):
        axis, by = link
        n = {"x": NX, "z": NZ, "y": NY, "core": NC}[axis]
        by %= n
        far = min(by, n - by)
        way = (axis, 1 if 2 * by <= n else -1)
        self.units[name] = dict(to=(axis, by), link=way, far=far, blocks=blocks, src=src, dst=dst, index=len(self.units))

    def step(self, name, fn=None, after=(), recv=(), send=(), cost=0.02, wave=0):
        self.steps[name] = dict(fn=fn, after=list(after), recv=list(recv), send=list(send), cost=cost, wave=wave)

    def order(self, block_bytes):
        sender = {u: s for s, v in self.steps.items() for u in v["send"]}
        needed = {s: [] for s in self.steps}
        for s, v in self.steps.items():
            for a in v["after"]:
                needed[a].append((s, 0.0))
            for u in v["recv"]:
                unit = self.units[u]
                needed[sender[u]].append((s, unit["blocks"] * block_bytes / LINK + HOP_US + FAR_US * (unit["far"] - 1)))
        path = {}

        def length(s):
            if s not in path:
                path[s] = self.steps[s]["cost"] + max([d + length(t) for t, d in needed[s]] + [0.0])
            return path[s]

        for s in self.steps:
            length(s)
        core, links, arrival, done, left, result = 0.0, {}, {}, {}, list(self.steps), []
        while left:
            best = None
            for s in left:
                v = self.steps[s]
                if any(a not in done for a in v["after"]) or any(u not in arrival for u in v["recv"]):
                    continue
                ready = max([done[a] for a in v["after"]] + [arrival[u] for u in v["recv"]] + [core])
                ahead = AHEAD_US if v["wave"] == 0 else LATER_US[0]
                begin = max([ready] + [links.get(self.units[u]["link"], 0.0) - ahead for u in v["send"]])
                key = (round((begin + LATER_US[1] * min(v["wave"], 1)) / 0.2), v["wave"], -path[s])
                if best is None or key < best[0]:
                    best = (key, s, ready)
            _, s, ready = best
            left.remove(s)
            result.append(s)
            core = ready + self.steps[s]["cost"]
            done[s] = core
            for u in self.steps[s]["send"]:
                link = self.units[u]["link"]
                rate = LINK if link[0] != "core" else 8 * LINK
                far = self.units[u]["far"]
                begin = max(core, links.get(link, 0.0))
                links[link] = begin + self.units[u]["blocks"] * far * block_bytes / rate
                arrival[u] = links[link] + HOP_US + FAR_US * (far - 1)
        self.total = core
        return result


def need_order():
    blocks, where, seg = [], {}, []
    for wave in range(max(WAVES) + 1):
        pair = [st for st in range(len(STREAMS)) if WAVES[st] == wave]
        rest = {st: [(off, sub) for off in offsets(sizes(STREAMS[st])[0]) for sub in range(subs_of(STREAMS[st]))] for st in pair}
        for st in pair:
            n = sizes(STREAMS[st])[0]
            rank = {o: min(o, n - o) for o in range(n)}
            if STREAMS[st] == "x":
                rest[st].sort(key=lambda u: (u[0] == 0, (rank[u[0]] != n // 2) * u[1], -rank[u[0]]))
        slots = 5
        for t in range(slots):
            begin = len(blocks)
            for st in pair:
                n, second = sizes(STREAMS[st])
                mine = rest[st]
                take = -(-len(mine) // (slots - t))
                for off, sub in mine[:take]:
                    where[st, off, sub] = (len(blocks), len(seg))
                    far = offsets(second)
                    width = second // subs_of(STREAMS[st])
                    for other in far[sub * width:(sub + 1) * width]:
                        blocks.append(((other, off) if STREAMS[st] == "z" else (off, other)) + (st,))
                rest[st] = mine[take:]
            seg.append((wave, begin, len(blocks)))
    return blocks, where, seg


def kernel(plan_only, group, used, table, lists, readers, seq, features, tiles, weight, hidden, ghosts, *scratch):
    feats, bank, mix, part, gy, g, gx, mixed, send_sem, recv_sem, local_sem = scratch[:11]
    per = [scratch[11 + 5 * st:16 + 5 * st] for st in range(len(STREAMS))]
    blocks, where, seg = need_order()
    plan = Plan()
    size = features.shape[1]
    rows = features.shape[0] // 4
    deep = tiles.shape[0]
    mid = rows // 2
    if not plan_only:
        edge, feat = lax.axis_index("edge"), lax.axis_index("feat")
        x, z, y, core = edge // NZ, edge % NZ, feat // NC, feat % NC
        peers = {}
        for axis, by in used:
            if axis == "x":
                peers[axis, by] = ((x + by) % NX * NZ + z, feat)
            elif axis == "z":
                peers[axis, by] = (x * NZ + (z + by) % NZ, feat)
            elif axis == "y":
                peers[axis, by] = (edge, (y + by) % NY * NC + core)
            else:
                peers[axis, by] = (edge, y * NC + (core + by) % NC)
        greeted = list(peers)
        barrier = pltpu.get_barrier_semaphore()
        for k in greeted:
            pl.semaphore_signal(barrier, inc=1, device_id=peers[k], device_id_type=MESH_ID)
        loads = [
            pltpu.make_async_copy(tiles, bank.at[pl.ds(0, deep)], local_sem.at[0]),
            pltpu.make_async_copy(features, feats, local_sem.at[1]),
        ]
        for ry in range(NY):
            row = (y + ry) % NY * NC * size
            loads.append(
                pltpu.make_async_copy(
                    weight.at[pl.ds(pl.multiple_of(row, size), NC * size)],
                    mix.at[pl.ds(ry * NC * size, NC * size)],
                    local_sem.at[2 + ry],
                )
            )
        for c in range(4):
            loads.append(pltpu.make_async_copy(features.at[pl.ds(c * rows, rows)], gx.at[c, 0, 0], local_sem.at[2 + NY + c]))
        for c in loads:
            c.start()
        bank[deep] = jnp.zeros_like(bank[deep])
        loads[0].wait()
        loads[1].wait()
        for c in loads[2 + NY:]:
            c.wait()

    def products(lo, hi, source):
        def body(i, carry):
            parts = []
            for b in range(group):
                v = seq[i * group + b]
                j = v % 4
                owner = (x + v // 1024) % NX * NZ + (z + v // 4 % 256) % NZ
                slot = jnp.int32(0)
                for c in range(4):
                    slot = slot + jnp.where(lists[owner * 4 + c] == j, c, 0)
                base = (owner * 4 + slot % 4) * 4
                parts.append(jnp.concatenate([bank[table[base + c]] for c in range(4)], axis=1))
            value = jnp.dot(jnp.concatenate(parts, axis=0), source[...], preferred_element_type=jnp.float32)
            part[pl.ds(i * group, group)] = value.reshape(group, rows, size)
            return carry

        lax.fori_loop(lo // group, hi // group, body, 0)

    for t, (wave, lo, hi) in enumerate(seg):
        pre = PRE[WAVES.index(wave)]
        plan.step(
            ("P", t), functools.partial(products, lo, hi, mixed if pre else feats), cost=GROUP_US * (hi - lo) / 4,
            after=([("P", t - 1)] if t else []) + ([("V", c) for c in range(4)] if pre else []), wave=wave,
        )

    def cut(half):
        return pl.ds(half * mid, mid)

    def total(count, own, extras, put):
        def body(k, carry):
            for half, more in extras:
                value = own(k, half)
                for e in more:
                    value = value + e(k, half).astype(jnp.float32)
                put(k, half, value)
            return carry

        lax.fori_loop(0, count, body, 0) if count > 1 else body(0, 0)

    def rows_of(s, d, n):
        hv = halves_of(s, d + 1, n)
        return pl.ds(hv[0] * mid, mid * len(hv)), len(hv) / 2

    def all_columns(key, ref, i, ready, wave):
        hy, arrivals = NY // 2, []
        if NC > 1:
            plan.unit(("YP", key, 0, 0), ("core", 1), 1, (ref, (i, 0, 0)), (ref, (i, 0, 1)))
            arrivals.append(("YP", key, 0, 0))
        for s in SIGNS:
            for d in range(hy):
                w, c = rows_of(s, d, NY)
                here, there = -s * d % NY, -s * (d + 1) % NY
                plan.unit(("Y", key, s, d), ("y", s), c, (ref, (i, here, 0, w)), (ref, (i, there, 0, w)))
                arrivals.append(("Y", key, s, d))
                if NC > 1:
                    plan.unit(("YP", key, s, d + 1), ("core", 1), c, (ref, (i, there, 0, w)), (ref, (i, there, 1, w)))
                    arrivals.append(("YP", key, s, d + 1))
        send = ([("Y", key, s, 0) for s in SIGNS] if NY > 1 else []) + ([("YP", key, 0, 0)] if NC > 1 else [])
        plan.step(("Y", key), after=ready, send=send, wave=wave)
        for s in SIGNS:
            for d in range(1, hy + 1):
                send = ([("Y", key, s, d)] if d < hy else []) + ([("YP", key, s, d)] if NC > 1 else [])
                plan.step(("Y", key, s, d), recv=[("Y", key, s, d - 1)], send=send, wave=wave)
        return arrivals

    def by_weight(ref, i, put):
        def wide(swap):
            order = [(ry, (rc + swap) % NC) for ry in range(NY) for rc in range(NC)]
            put(jnp.dot(jnp.concatenate([ref[i, ry, rc] for ry, rc in order], axis=1), mix[...], preferred_element_type=jnp.float32))

        for c in range(NC):
            pl.when(core == c)(functools.partial(wide, c))

    for c in range(4) if any(PRE) else ():
        arrivals = all_columns(("X", c), gx, c, [("P", 0)], 0)

        def put(value, c=c):
            mixed[pl.ds(c * rows, rows)] = value.astype(jnp.bfloat16)

        plan.step(("V", c), functools.partial(by_weight, gx, c, put), after=[("W",), ("Y", ("X", c))], recv=arrivals, cost=0.5)

    everything = []
    for st, kind in enumerate(STREAMS):
        wave = WAVES[st]
        n1, n2 = sizes(kind)
        a1, a2 = ("z", "x") if kind == "z" else ("x", "z")
        h1, h2, hy = n1 // 2, n2 // 2, NY // 2
        subs = subs_of(kind)
        width = n2 // subs
        off2 = offsets(n2)
        s1, r1, s2, r2, q = per[st]

        def unit1(s, r, sub, ref, st=st, width=width, n1=n1):
            hv = halves_of(s, r, n1)
            return ref, (lead(s), r - 1, pl.ds(sub * width, width), pl.ds(hv[0] * mid, mid * len(hv)))

        for s in SIGNS:
            for r in range(1, h1 + 1):
                for sub in range(subs):
                    plan.unit(("A", st, s, r, sub), (a1, s), width * len(halves_of(s, r, n1)) / 2, unit1(s, r, sub, s1), unit1(s, r, sub, r1))

        def in1(s, r, sub, k, half, r1=r1, width=width):
            return r1[lead(s), r - 1, sub * width + k, cut(half)]

        for s in SIGNS:
            for r in range(h1, 0, -1):
                for sub in range(subs):
                    base, t = where[st, s * r % n1, sub]

                    def own(k, half, base=base):
                        return part[base + k, cut(half)]

                    def put(k, half, value, s=s, r=r, sub=sub, s1=s1, width=width):
                        s1[lead(s), r - 1, sub * width + k, cut(half)] = value.astype(jnp.bfloat16)

                    extras = [
                        (half, [functools.partial(in1, s, r + 1, sub)] if half in halves_of(s, r + 1, n1) else [])
                        for half in halves_of(s, r, n1)
                    ]
                    plan.step(
                        ("A", st, s, r, sub), functools.partial(total, width, own, extras, put), after=[("P", t)],
                        recv=[("A", st, s, r + 1, sub)] if r < h1 else [], send=[("A", st, s, r, sub)], cost=0.15, wave=wave,
                    )
        for sub in range(subs):
            base, t = where[st, 0, sub]

            def own(k, half, base=base):
                return part[base + k, cut(half)]

            def put(k, half, value, sub=sub, q=q, width=width):
                q[sub * width + k, cut(half)] = value

            extras = [(half, [functools.partial(in1, s, 1, sub) for s in SIGNS if half in halves_of(s, 1, n1)]) for half in (0, 1)]
            plan.step(
                ("Af", st, sub), functools.partial(total, width, own, extras, put), after=[("P", t)],
                recv=[("A", st, s, 1, sub) for s in SIGNS] if n1 > 1 else [], cost=0.15, wave=wave,
            )

        if a2 in DIRECT["B"]:
            for o in off2[:-1]:
                plan.unit(("B", st, o), (a2, o), 1, (s2, (o - 1,)), (r2, (o - 1,)))
                p = off2.index(o)

                def own(k, half, p=p, q=q):
                    return q[p, cut(half)]

                def put(k, half, value, o=o, s2=s2):
                    s2[o - 1, cut(half)] = value.astype(jnp.bfloat16)

                plan.step(
                    ("B", st, o), functools.partial(total, 1, own, [(0, []), (1, [])], put), after=[("Af", st, p // width)],
                    send=[("B", st, o)], cost=0.06, wave=wave,
                )

            def come(o, k, half, r2=r2):
                return r2[o - 1, cut(half)]

            last = [(half, [functools.partial(come, o) for o in off2[:-1]]) for half in (0, 1)]
            last_recv = [("B", st, o) for o in off2[:-1]]
        else:
            def unit2(s, r, ref, n2=n2):
                hv = halves_of(s, r, n2)
                return ref, (lead(s), r - 1, pl.ds(hv[0] * mid, mid * len(hv)))

            for s in SIGNS:
                for r in range(1, h2 + 1):
                    plan.unit(("B", st, s, r), (a2, s), len(halves_of(s, r, n2)) / 2, unit2(s, r, s2), unit2(s, r, r2))

            def in2(s, r, k, half, r2=r2):
                return r2[lead(s), r - 1, cut(half)]

            for s in SIGNS:
                for r in range(h2, 0, -1):
                    p = off2.index(s * r % n2)

                    def own(k, half, p=p, q=q):
                        return q[p, cut(half)]

                    def put(k, half, value, s=s, r=r, s2=s2):
                        s2[lead(s), r - 1, cut(half)] = value.astype(jnp.bfloat16)

                    extras = [
                        (half, [functools.partial(in2, s, r + 1)] if half in halves_of(s, r + 1, n2) else []) for half in halves_of(s, r, n2)
                    ]
                    plan.step(
                        ("B", st, s, r), functools.partial(total, 1, own, extras, put), after=[("Af", st, p // width)],
                        recv=[("B", st, s, r + 1)] if r < h2 else [], send=[("B", st, s, r)], cost=0.06, wave=wave,
                    )

            last = [(half, [functools.partial(in2, s, 1) for s in SIGNS if half in halves_of(s, 1, n2)]) for half in (0, 1)]
            last_recv = [("B", st, s, 1) for s in SIGNS] if n2 > 1 else []
        p = off2.index(0)

        def own(k, half, p=p, q=q):
            return q[p, cut(half)]

        def put(k, half, value, st=st):
            if PRE[st]:
                value = jnp.maximum(value, 0.0).astype(jnp.bfloat16)
                g[st * NX * NZ, cut(half)] = value
                hidden[pl.ds(st * rows + half * mid, mid)] = value
            else:
                gy[st, 0, 0, cut(half)] = value.astype(jnp.bfloat16)

        plan.step(
            ("Bf", st), functools.partial(total, 1, own, last, put), after=[("Af", st, p // width)],
            recv=last_recv, cost=0.06, wave=wave,
        )

        if not PRE[st]:
            arrivals = all_columns(st, gy, st, [("Bf", st)], wave)

        a1, a2 = (("z", "x"), ("x", "z"))[FIRST[st] == "x"]
        n1, n2 = {"z": NZ, "x": NX}[a1], {"z": NZ, "x": NX}[a2]
        h1, h2 = n1 // 2, n2 // 2

        def slot(qpos, q2, st=st, n1=n1):
            return st * NX * NZ + q2 * n1 + qpos

        def finish(value, st=st):
            value = jnp.maximum(value, 0.0).astype(jnp.bfloat16)
            g[st * NX * NZ] = value
            hidden[pl.ds(st * rows, rows)] = value

        if PRE[st]:
            plan.step(("H", st), after=[("Bf", st)], wave=wave)
        else:
            plan.step(
                ("H", st), functools.partial(by_weight, gy, st, finish), after=[("W",), ("Y", st)], recv=arrivals, cost=0.5, wave=wave
            )

        back1 = offsets(n1)[::-1]
        where1 = {o: i for i, o in enumerate(back1)}
        sets = groups_of(n1)
        for o in range(1, n1) if a1 in DIRECT["C"] else ():
            plan.unit(("C", st, o), (a1, o), 1, (g, (slot(0, 0),)), (g, (slot(where1[-o % n1], 0),)))
            everything.append(("C", st, o))
        for s in SIGNS if a1 not in DIRECT["C"] else ():
            for d in range(h1):
                w, c = rows_of(s, d, n1)
                plan.unit(
                    ("C", st, s, d), (a1, s), c, (g, (slot(where1[-s * d % n1], 0), w)), (g, (slot(where1[-s * (d + 1) % n1], 0), w))
                )
                everything.append(("C", st, s, d))
        for i, members in enumerate(sets):
            for s in SIGNS:
                for d in range(h2):
                    w, c = rows_of(s, d, n2)
                    here = pl.ds(slot(members[0], -s * d % n2), len(members))
                    there = pl.ds(slot(members[0], -s * (d + 1) % n2), len(members))
                    plan.unit(("D", st, i, s, d), (a2, s), c * len(members), (g, (here, w)), (g, (there, w)))
                    everything.append(("D", st, i, s, d))
        second = lambda i: [("D", st, i, s, 0) for s in SIGNS] if h2 else []
        if a1 in DIRECT["C"]:
            far = sorted(range(1, n1), key=lambda o: -min(o, n1 - o))
            plan.step(("C", st), after=[("H", st)], send=[("C", st, o) for o in far], wave=wave)
            for d in range(1, h1 + 1):
                plan.step(("D", st, d), recv=[("C", st, o) for o in sorted({d, n1 - d})], send=second(d), wave=wave)
        else:
            plan.step(("C", st), after=[("H", st)], send=[("C", st, s, 0) for s in SIGNS] if h1 else [], wave=wave)
        plan.step(("D", st, 0), after=[("H", st)], send=second(0), wave=wave)
        for d in range(1, h1 + 1) if a1 not in DIRECT["C"] else ():
            for s in SIGNS:
                if d < h1:
                    plan.step(("C", st, s, d), recv=[("C", st, s, d - 1)], send=[("C", st, s, d)], wave=wave)
            plan.step(("D", st, d), recv=[("C", st, s, d - 1) for s in SIGNS], send=second(d), wave=wave)
        for i in range(len(sets)):
            for s in SIGNS:
                for d in range(1, h2):
                    plan.step(("D", st, i, s, d), recv=[("D", st, i, s, d - 1)], send=[("D", st, i, s, d)], wave=wave)

    def weights():
        for c in loads[2:2 + NY]:
            c.wait()

    plan.step(("W",), weights, after=[("P", 0)])

    def place(q, n):
        return jnp.where(2 * q < n, 2 * q, 2 * (n - q) - 1) % n

    def gather():
        def body(r, carry):
            v = readers[r]
            o, j = v // 4, v % 4
            rx, rz = (o // NZ - x + NX) % NX, (o % NZ - z + NZ) % NZ
            first_z = j < 0
            for st, axis in enumerate(FIRST):
                if axis == "z":
                    first_z = jnp.logical_or(first_z, j == st)
            at = j * NX * NZ + jnp.where(first_z, rx * NZ + place(rz, NZ), rz * NX + place(rx, NX))
            ghosts[pl.ds(pl.multiple_of(r * rows, rows), rows)] = g[at]
            return carry

        lax.fori_loop(0, readers.shape[0], body, 0)

    plan.step(("G",), gather, after=[("H", st) for st in range(len(STREAMS))], recv=everything, cost=0.5, wave=9)

    order = plan.order(rows * size * 2)
    if plan_only:
        return plan, order

    def copy(name):
        u = plan.units[name]
        (sref, sat), (dref, dat) = u["src"], u["dst"]
        return pltpu.make_async_remote_copy(
            src_ref=sref.at[sat], dst_ref=dref.at[dat], send_sem=send_sem.at[u["index"]], recv_sem=recv_sem.at[u["index"]],
            device_id=peers[u["to"]], device_id_type=MESH_ID,
        )

    copies = {name: copy(name) for name in plan.units}
    arrived, opened = set(), False
    for name in order:
        step = plan.steps[name]
        for u in step["recv"]:
            if u not in arrived:
                copies[u].wait_recv()
                arrived.add(u)
        if step["fn"] is not None:
            step["fn"]()
        if step["send"] and not opened:
            pl.semaphore_wait(barrier, len(greeted))
            opened = True
        for u in step["send"]:
            copies[u].start()
    for name in plan.units:
        if name not in arrived:
            copies[name].wait_recv()
        copies[name].wait_send()


def scratch_shapes(rows, size, deep, count):
    bf, fp, v = jnp.bfloat16, jnp.float32, pltpu.VMEM
    blocks, where, seg = need_order()
    shapes = [
        v((4 * rows, size), bf), v((deep + 1, rows, rows), bf), v((NY * NC * size, size), bf), v((len(blocks), rows, size), fp),
        v((len(STREAMS), NY, NC, rows, size), bf), v((len(STREAMS) * NX * NZ, rows, size), bf),
        v((4, NY, NC, rows, size), bf), v((4 * rows, size), bf),
        pltpu.SemaphoreType.DMA((count,)), pltpu.SemaphoreType.DMA((count,)), pltpu.SemaphoreType.DMA((6 + NY,)),
    ]
    for kind in STREAMS:
        n1, n2 = sizes(kind)
        first, second = v((2, max(n1 // 2, 1), n2, rows, size), bf), v((2, max(n2 // 2, 1), rows, size), bf)
        if {"z": "x", "x": "z"}[kind] in DIRECT["B"]:
            second = v((max(n2 - 1, 1), rows, size), bf)
        shapes += [first, first, second, second, v((n2, rows, size), fp)]
    return shapes


def local(features, tiles, tile_slot, tile_col, tile_id, touched, weight, readers):
    edge = lax.axis_index("edge")
    block = tiles.shape[1]
    size = features.shape[1]
    deep = tiles.shape[0]
    blocks, where, seg = need_order()
    group = 4 if all((hi - lo) % 4 == 0 for _, lo, hi in seg) else 1
    seq = jnp.array([rx * 1024 + rz * 4 + j for rx, rz, j in blocks], jnp.int32)
    lists = lax.dynamic_index_in_dim(touched, edge, 0, keepdims=False).reshape(-1)
    keys = jnp.arange(lists.shape[0] * 4, dtype=jnp.int32)
    pair = tile_slot * 4 + tile_col
    table = deep + jnp.sum(jnp.where(keys[:, None] == pair[None, :], tile_id[None, :] - deep, 0), axis=1)
    args = (table.astype(jnp.int32), lists, readers, seq, features, tiles, weight)
    plan, order = kernel(True, group, None, *args, None, None, *([None] * 31))
    used = sorted({u["to"] for u in plan.units.values()} | {(u["to"][0], -u["to"][1] % {"x": NX, "z": NZ, "y": NY, "core": NC}[u["to"][0]]) for u in plan.units.values()})
    vmem = pl.BlockSpec(memory_space=pltpu.VMEM)
    smem = pl.BlockSpec(memory_space=pltpu.SMEM)
    hbm = pl.BlockSpec(memory_space=pltpu.HBM)
    return pl.pallas_call(
        functools.partial(kernel, False, group, used),
        out_shape=(
            jax.ShapeDtypeStruct(features.shape, jnp.bfloat16),
            jax.ShapeDtypeStruct((readers.shape[0] * block, size), jnp.bfloat16),
        ),
        in_specs=[smem, smem, smem, smem, hbm, hbm, hbm],
        out_specs=(vmem, vmem),
        scratch_shapes=scratch_shapes(block, size, deep, len(plan.units)),
        compiler_params=pltpu.CompilerParams(collective_id=0, has_side_effects=True, vmem_limit_bytes=52 << 20),
        name="layer",
    )(*args)


def solution(mesh):
    in_specs = (
        P("edge", "feat"),
        P("edge", None, None),
        P("edge"),
        P("edge"),
        P("edge"),
        P(),
        P(None, "feat"),
        P("edge"),
    )
    out_specs = (P("edge", "feat"), P("edge", "feat"))
    return jax.shard_map(local, mesh=mesh, in_specs=in_specs, out_specs=out_specs, check_vma=False)
```

```python
import functools

import jax
import jax.numpy as jnp
import numpy as np
from jax import lax
from jax.experimental import pallas as pl
from jax.experimental.pallas import tpu as pltpu
from jax.sharding import PartitionSpec as P

NX, NZ, NY, NC = 4, 8, 8, 2
STREAMS = ("x", "z", "x", "z")
PRE = (False, False, True, True)
WAVES = (0, 0, 1, 1)
FIRST = ('x', 'z', 'x', 'z')
DIRECT = {"B": (), "C": (), "Y": False}
SUBS = {'z': 2, 'x': 4}
HOP_US, LINK, GROUP_US, AHEAD_US, FAR_US = 2.3, 46.5e3, 0.3, 0.5, 0.8
LATER_US = (1.5, 0.0)
MESH_ID = pl.DeviceIdType.MESH
SIGNS = (1, -1)


def offsets(n):
    h = n // 2
    out = [h] if n > 1 else []
    for r in range(h - 1, 0, -1):
        out += [r, n - r]
    return out + [0]


def groups_of(n):
    h = n // 2
    out, at = [[0]], 1
    for d in range(1, h + 1):
        count = 1 if 2 * d == n else 2
        out.append(list(range(at, at + count)))
        at += count
    return out


def lead(sign):
    return 0 if sign > 0 else 1


def halves_of(sign, r, n):
    if not 1 <= r <= n // 2:
        return []
    return [lead(sign)] if r == n // 2 else [0, 1]


def sizes(kind):
    return (NZ, NX) if kind == "z" else (NX, NZ)


def subs_of(kind):
    return SUBS[kind] if sizes(kind)[1] >= 4 else 1


class Plan:
    def __init__(self):
        self.steps = {}
        self.units = {}

    def unit(self, name, link, blocks, src, dst):
        axis, by = link
        n = {"x": NX, "z": NZ, "y": NY, "core": NC}[axis]
        by %= n
        far = min(by, n - by)
        way = (axis, 1 if 2 * by <= n else -1)
        self.units[name] = dict(to=(axis, by), link=way, far=far, blocks=blocks, src=src, dst=dst, index=len(self.units))

    def step(self, name, fn=None, after=(), recv=(), send=(), cost=0.02, wave=0):
        self.steps[name] = dict(fn=fn, after=list(after), recv=list(recv), send=list(send), cost=cost, wave=wave)

    def order(self, block_bytes):
        sender = {u: s for s, v in self.steps.items() for u in v["send"]}
        needed = {s: [] for s in self.steps}
        for s, v in self.steps.items():
            for a in v["after"]:
                needed[a].append((s, 0.0))
            for u in v["recv"]:
                unit = self.units[u]
                needed[sender[u]].append((s, unit["blocks"] * block_bytes / LINK + HOP_US + FAR_US * (unit["far"] - 1)))
        path = {}

        def length(s):
            if s not in path:
                path[s] = self.steps[s]["cost"] + max([d + length(t) for t, d in needed[s]] + [0.0])
            return path[s]

        for s in self.steps:
            length(s)
        core, links, arrival, done, left, result = 0.0, {}, {}, {}, list(self.steps), []
        while left:
            best = None
            for s in left:
                v = self.steps[s]
                if any(a not in done for a in v["after"]) or any(u not in arrival for u in v["recv"]):
                    continue
                ready = max([done[a] for a in v["after"]] + [arrival[u] for u in v["recv"]] + [core])
                ahead = AHEAD_US if v["wave"] == 0 else LATER_US[0]
                begin = max([ready] + [links.get(self.units[u]["link"], 0.0) - ahead for u in v["send"]])
                key = (round((begin + LATER_US[1] * min(v["wave"], 1)) / 0.2), v["wave"], -path[s])
                if best is None or key < best[0]:
                    best = (key, s, ready)
            _, s, ready = best
            left.remove(s)
            result.append(s)
            core = ready + self.steps[s]["cost"]
            done[s] = core
            for u in self.steps[s]["send"]:
                link = self.units[u]["link"]
                rate = LINK if link[0] != "core" else 8 * LINK
                far = self.units[u]["far"]
                begin = max(core, links.get(link, 0.0))
                links[link] = begin + self.units[u]["blocks"] * far * block_bytes / rate
                arrival[u] = links[link] + HOP_US + FAR_US * (far - 1)
        self.total = core
        return result


def need_order():
    blocks, where, seg = [], {}, []
    for wave in range(max(WAVES) + 1):
        pair = [st for st in range(len(STREAMS)) if WAVES[st] == wave]
        rest = {st: [(off, sub) for off in offsets(sizes(STREAMS[st])[0]) for sub in range(subs_of(STREAMS[st]))] for st in pair}
        for st in pair:
            n = sizes(STREAMS[st])[0]
            rank = {o: min(o, n - o) for o in range(n)}
            if STREAMS[st] == "x":
                rest[st].sort(key=lambda u: (u[0] == 0, (rank[u[0]] != n // 2) * u[1], -rank[u[0]]))
        slots = 8
        for t in range(slots):
            begin = len(blocks)
            for st in pair:
                n, second = sizes(STREAMS[st])
                mine = rest[st]
                take = -(-len(mine) // (slots - t))
                for off, sub in mine[:take]:
                    where[st, off, sub] = (len(blocks), len(seg))
                    far = offsets(second)
                    width = second // subs_of(STREAMS[st])
                    for other in far[sub * width:(sub + 1) * width]:
                        blocks.append(((other, off) if STREAMS[st] == "z" else (off, other)) + (st,))
                rest[st] = mine[take:]
            seg.append((wave, begin, len(blocks)))
    return blocks, where, seg


def kernel(plan_only, group, used, table, lists, readers, seq, features, tiles, weight, hidden, ghosts, *scratch):
    feats, bank, mix, part, gy, g, gx, mixed, send_sem, recv_sem, local_sem = scratch[:11]
    per = [scratch[11 + 5 * st:16 + 5 * st] for st in range(len(STREAMS))]
    blocks, where, seg = need_order()
    plan = Plan()
    size = features.shape[1]
    rows = features.shape[0] // 4
    deep = tiles.shape[0]
    mid = rows // 2
    if not plan_only:
        edge, feat = lax.axis_index("edge"), lax.axis_index("feat")
        x, z, y, core = edge // NZ, edge % NZ, feat // NC, feat % NC
        peers = {}
        for axis, by in used:
            if axis == "x":
                peers[axis, by] = ((x + by) % NX * NZ + z, feat)
            elif axis == "z":
                peers[axis, by] = (x * NZ + (z + by) % NZ, feat)
            elif axis == "y":
                peers[axis, by] = (edge, (y + by) % NY * NC + core)
            else:
                peers[axis, by] = (edge, y * NC + (core + by) % NC)
        greeted = list(peers)
        barrier = pltpu.get_barrier_semaphore()
        for k in greeted:
            pl.semaphore_signal(barrier, inc=1, device_id=peers[k], device_id_type=MESH_ID)
        loads = [
            pltpu.make_async_copy(tiles, bank.at[pl.ds(0, deep)], local_sem.at[0]),
            pltpu.make_async_copy(features, feats, local_sem.at[1]),
        ]
        for ry in range(NY):
            row = (y + ry) % NY * NC * size
            loads.append(
                pltpu.make_async_copy(
                    weight.at[pl.ds(pl.multiple_of(row, size), NC * size)],
                    mix.at[pl.ds(ry * NC * size, NC * size)],
                    local_sem.at[2 + ry],
                )
            )
        for c in range(4):
            loads.append(pltpu.make_async_copy(features.at[pl.ds(c * rows, rows)], gx.at[c, 0, 0], local_sem.at[2 + NY + c]))
        for c in loads:
            c.start()
        bank[deep] = jnp.zeros_like(bank[deep])
        loads[0].wait()
        loads[1].wait()
        for c in loads[2 + NY:]:
            c.wait()

    def products(lo, hi, source):
        def body(i, carry):
            parts = []
            for b in range(group):
                v = seq[i * group + b]
                j = v % 4
                owner = (x + v // 1024) % NX * NZ + (z + v // 4 % 256) % NZ
                slot = jnp.int32(0)
                for c in range(4):
                    slot = slot + jnp.where(lists[owner * 4 + c] == j, c, 0)
                base = (owner * 4 + slot % 4) * 4
                parts.append(jnp.concatenate([bank[table[base + c]] for c in range(4)], axis=1))
            value = jnp.dot(jnp.concatenate(parts, axis=0), source[...], preferred_element_type=jnp.float32)
            part[pl.ds(i * group, group)] = value.reshape(group, rows, size)
            return carry

        lax.fori_loop(lo // group, hi // group, body, 0)

    for t, (wave, lo, hi) in enumerate(seg):
        pre = PRE[WAVES.index(wave)]
        plan.step(
            ("P", t), functools.partial(products, lo, hi, mixed if pre else feats), cost=GROUP_US * (hi - lo) / 4,
            after=([("P", t - 1)] if t else []) + ([("V", c) for c in range(4)] if pre else []), wave=wave,
        )

    def cut(half):
        return pl.ds(half * mid, mid)

    def total(count, own, extras, put):
        def body(k, carry):
            for half, more in extras:
                value = own(k, half)
                for e in more:
                    value = value + e(k, half).astype(jnp.float32)
                put(k, half, value)
            return carry

        lax.fori_loop(0, count, body, 0) if count > 1 else body(0, 0)

    def rows_of(s, d, n):
        hv = halves_of(s, d + 1, n)
        return pl.ds(hv[0] * mid, mid * len(hv)), len(hv) / 2

    def all_columns(key, ref, i, ready, wave):
        hy, arrivals = NY // 2, []
        if NC > 1:
            plan.unit(("YP", key, 0, 0), ("core", 1), 1, (ref, (i, 0, 0)), (ref, (i, 0, 1)))
            arrivals.append(("YP", key, 0, 0))
        for s in SIGNS:
            for d in range(hy):
                w, c = rows_of(s, d, NY)
                here, there = -s * d % NY, -s * (d + 1) % NY
                plan.unit(("Y", key, s, d), ("y", s), c, (ref, (i, here, 0, w)), (ref, (i, there, 0, w)))
                arrivals.append(("Y", key, s, d))
                if NC > 1:
                    plan.unit(("YP", key, s, d + 1), ("core", 1), c, (ref, (i, there, 0, w)), (ref, (i, there, 1, w)))
                    arrivals.append(("YP", key, s, d + 1))
        send = ([("Y", key, s, 0) for s in SIGNS] if NY > 1 else []) + ([("YP", key, 0, 0)] if NC > 1 else [])
        plan.step(("Y", key), after=ready, send=send, wave=wave)
        for s in SIGNS:
            for d in range(1, hy + 1):
                send = ([("Y", key, s, d)] if d < hy else []) + ([("YP", key, s, d)] if NC > 1 else [])
                plan.step(("Y", key, s, d), recv=[("Y", key, s, d - 1)], send=send, wave=wave)
        return arrivals

    def by_weight(ref, i, put):
        def wide(swap):
            order = [(ry, (rc + swap) % NC) for ry in range(NY) for rc in range(NC)]
            put(jnp.dot(jnp.concatenate([ref[i, ry, rc] for ry, rc in order], axis=1), mix[...], preferred_element_type=jnp.float32))

        for c in range(NC):
            pl.when(core == c)(functools.partial(wide, c))

    for c in range(4) if any(PRE) else ():
        arrivals = all_columns(("X", c), gx, c, [("P", 0)], 0)

        def put(value, c=c):
            mixed[pl.ds(c * rows, rows)] = value.astype(jnp.bfloat16)

        plan.step(("V", c), functools.partial(by_weight, gx, c, put), after=[("W",), ("Y", ("X", c))], recv=arrivals, cost=0.5)

    everything = []
    for st, kind in enumerate(STREAMS):
        wave = WAVES[st]
        n1, n2 = sizes(kind)
        a1, a2 = ("z", "x") if kind == "z" else ("x", "z")
        h1, h2, hy = n1 // 2, n2 // 2, NY // 2
        subs = subs_of(kind)
        width = n2 // subs
        off2 = offsets(n2)
        s1, r1, s2, r2, q = per[st]

        def unit1(s, r, sub, ref, st=st, width=width, n1=n1):
            hv = halves_of(s, r, n1)
            return ref, (lead(s), r - 1, pl.ds(sub * width, width), pl.ds(hv[0] * mid, mid * len(hv)))

        for s in SIGNS:
            for r in range(1, h1 + 1):
                for sub in range(subs):
                    plan.unit(("A", st, s, r, sub), (a1, s), width * len(halves_of(s, r, n1)) / 2, unit1(s, r, sub, s1), unit1(s, r, sub, r1))

        def in1(s, r, sub, k, half, r1=r1, width=width):
            return r1[lead(s), r - 1, sub * width + k, cut(half)]

        for s in SIGNS:
            for r in range(h1, 0, -1):
                for sub in range(subs):
                    base, t = where[st, s * r % n1, sub]

                    def own(k, half, base=base):
                        return part[base + k, cut(half)]

                    def put(k, half, value, s=s, r=r, sub=sub, s1=s1, width=width):
                        s1[lead(s), r - 1, sub * width + k, cut(half)] = value.astype(jnp.bfloat16)

                    extras = [
                        (half, [functools.partial(in1, s, r + 1, sub)] if half in halves_of(s, r + 1, n1) else [])
                        for half in halves_of(s, r, n1)
                    ]
                    plan.step(
                        ("A", st, s, r, sub), functools.partial(total, width, own, extras, put), after=[("P", t)],
                        recv=[("A", st, s, r + 1, sub)] if r < h1 else [], send=[("A", st, s, r, sub)], cost=0.15, wave=wave,
                    )
        for sub in range(subs):
            base, t = where[st, 0, sub]

            def own(k, half, base=base):
                return part[base + k, cut(half)]

            def put(k, half, value, sub=sub, q=q, width=width):
                q[sub * width + k, cut(half)] = value

            extras = [(half, [functools.partial(in1, s, 1, sub) for s in SIGNS if half in halves_of(s, 1, n1)]) for half in (0, 1)]
            plan.step(
                ("Af", st, sub), functools.partial(total, width, own, extras, put), after=[("P", t)],
                recv=[("A", st, s, 1, sub) for s in SIGNS] if n1 > 1 else [], cost=0.15, wave=wave,
            )

        if a2 in DIRECT["B"]:
            for o in off2[:-1]:
                plan.unit(("B", st, o), (a2, o), 1, (s2, (o - 1,)), (r2, (o - 1,)))
                p = off2.index(o)

                def own(k, half, p=p, q=q):
                    return q[p, cut(half)]

                def put(k, half, value, o=o, s2=s2):
                    s2[o - 1, cut(half)] = value.astype(jnp.bfloat16)

                plan.step(
                    ("B", st, o), functools.partial(total, 1, own, [(0, []), (1, [])], put), after=[("Af", st, p // width)],
                    send=[("B", st, o)], cost=0.06, wave=wave,
                )

            def come(o, k, half, r2=r2):
                return r2[o - 1, cut(half)]

            last = [(half, [functools.partial(come, o) for o in off2[:-1]]) for half in (0, 1)]
            last_recv = [("B", st, o) for o in off2[:-1]]
        else:
            def unit2(s, r, ref, n2=n2):
                hv = halves_of(s, r, n2)
                return ref, (lead(s), r - 1, pl.ds(hv[0] * mid, mid * len(hv)))

            for s in SIGNS:
                for r in range(1, h2 + 1):
                    plan.unit(("B", st, s, r), (a2, s), len(halves_of(s, r, n2)) / 2, unit2(s, r, s2), unit2(s, r, r2))

            def in2(s, r, k, half, r2=r2):
                return r2[lead(s), r - 1, cut(half)]

            for s in SIGNS:
                for r in range(h2, 0, -1):
                    p = off2.index(s * r % n2)

                    def own(k, half, p=p, q=q):
                        return q[p, cut(half)]

                    def put(k, half, value, s=s, r=r, s2=s2):
                        s2[lead(s), r - 1, cut(half)] = value.astype(jnp.bfloat16)

                    extras = [
                        (half, [functools.partial(in2, s, r + 1)] if half in halves_of(s, r + 1, n2) else []) for half in halves_of(s, r, n2)
                    ]
                    plan.step(
                        ("B", st, s, r), functools.partial(total, 1, own, extras, put), after=[("Af", st, p // width)],
                        recv=[("B", st, s, r + 1)] if r < h2 else [], send=[("B", st, s, r)], cost=0.06, wave=wave,
                    )

            last = [(half, [functools.partial(in2, s, 1) for s in SIGNS if half in halves_of(s, 1, n2)]) for half in (0, 1)]
            last_recv = [("B", st, s, 1) for s in SIGNS] if n2 > 1 else []
        p = off2.index(0)

        def own(k, half, p=p, q=q):
            return q[p, cut(half)]

        def put(k, half, value, st=st):
            if PRE[st]:
                value = jnp.maximum(value, 0.0).astype(jnp.bfloat16)
                g[st * NX * NZ, cut(half)] = value
                hidden[pl.ds(st * rows + half * mid, mid)] = value
            else:
                gy[st, 0, 0, cut(half)] = value.astype(jnp.bfloat16)

        plan.step(
            ("Bf", st), functools.partial(total, 1, own, last, put), after=[("Af", st, p // width)],
            recv=last_recv, cost=0.06, wave=wave,
        )

        if not PRE[st]:
            arrivals = all_columns(st, gy, st, [("Bf", st)], wave)

        a1, a2 = (("z", "x"), ("x", "z"))[FIRST[st] == "x"]
        n1, n2 = {"z": NZ, "x": NX}[a1], {"z": NZ, "x": NX}[a2]
        h1, h2 = n1 // 2, n2 // 2

        def slot(qpos, q2, st=st, n1=n1):
            return st * NX * NZ + q2 * n1 + qpos

        def finish(value, st=st):
            value = jnp.maximum(value, 0.0).astype(jnp.bfloat16)
            g[st * NX * NZ] = value
            hidden[pl.ds(st * rows, rows)] = value

        if PRE[st]:
            plan.step(("H", st), after=[("Bf", st)], wave=wave)
        else:
            plan.step(
                ("H", st), functools.partial(by_weight, gy, st, finish), after=[("W",), ("Y", st)], recv=arrivals, cost=0.5, wave=wave
            )

        back1 = offsets(n1)[::-1]
        where1 = {o: i for i, o in enumerate(back1)}
        sets = groups_of(n1)
        for o in range(1, n1) if a1 in DIRECT["C"] else ():
            plan.unit(("C", st, o), (a1, o), 1, (g, (slot(0, 0),)), (g, (slot(where1[-o % n1], 0),)))
            everything.append(("C", st, o))
        for s in SIGNS if a1 not in DIRECT["C"] else ():
            for d in range(h1):
                w, c = rows_of(s, d, n1)
                plan.unit(
                    ("C", st, s, d), (a1, s), c, (g, (slot(where1[-s * d % n1], 0), w)), (g, (slot(where1[-s * (d + 1) % n1], 0), w))
                )
                everything.append(("C", st, s, d))
        for i, members in enumerate(sets):
            for s in SIGNS:
                for d in range(h2):
                    w, c = rows_of(s, d, n2)
                    here = pl.ds(slot(members[0], -s * d % n2), len(members))
                    there = pl.ds(slot(members[0], -s * (d + 1) % n2), len(members))
                    plan.unit(("D", st, i, s, d), (a2, s), c * len(members), (g, (here, w)), (g, (there, w)))
                    everything.append(("D", st, i, s, d))
        second = lambda i: [("D", st, i, s, 0) for s in SIGNS] if h2 else []
        if a1 in DIRECT["C"]:
            far = sorted(range(1, n1), key=lambda o: -min(o, n1 - o))
            plan.step(("C", st), after=[("H", st)], send=[("C", st, o) for o in far], wave=wave)
            for d in range(1, h1 + 1):
                plan.step(("D", st, d), recv=[("C", st, o) for o in sorted({d, n1 - d})], send=second(d), wave=wave)
        else:
            plan.step(("C", st), after=[("H", st)], send=[("C", st, s, 0) for s in SIGNS] if h1 else [], wave=wave)
        plan.step(("D", st, 0), after=[("H", st)], send=second(0), wave=wave)
        for d in range(1, h1 + 1) if a1 not in DIRECT["C"] else ():
            for s in SIGNS:
                if d < h1:
                    plan.step(("C", st, s, d), recv=[("C", st, s, d - 1)], send=[("C", st, s, d)], wave=wave)
            plan.step(("D", st, d), recv=[("C", st, s, d - 1) for s in SIGNS], send=second(d), wave=wave)
        for i in range(len(sets)):
            for s in SIGNS:
                for d in range(1, h2):
                    plan.step(("D", st, i, s, d), recv=[("D", st, i, s, d - 1)], send=[("D", st, i, s, d)], wave=wave)

    def weights():
        for c in loads[2:2 + NY]:
            c.wait()

    plan.step(("W",), weights, after=[("P", 0)])

    def place(q, n):
        return jnp.where(2 * q < n, 2 * q, 2 * (n - q) - 1) % n

    def gather():
        def body(r, carry):
            v = readers[r]
            o, j = v // 4, v % 4
            rx, rz = (o // NZ - x + NX) % NX, (o % NZ - z + NZ) % NZ
            first_z = j < 0
            for st, axis in enumerate(FIRST):
                if axis == "z":
                    first_z = jnp.logical_or(first_z, j == st)
            at = j * NX * NZ + jnp.where(first_z, rx * NZ + place(rz, NZ), rz * NX + place(rx, NX))
            ghosts[pl.ds(pl.multiple_of(r * rows, rows), rows)] = g[at]
            return carry

        lax.fori_loop(0, readers.shape[0], body, 0)

    plan.step(("G",), gather, after=[("H", st) for st in range(len(STREAMS))], recv=everything, cost=0.5, wave=9)

    order = plan.order(rows * size * 2)
    if plan_only:
        return plan, order

    def copy(name):
        u = plan.units[name]
        (sref, sat), (dref, dat) = u["src"], u["dst"]
        return pltpu.make_async_remote_copy(
            src_ref=sref.at[sat], dst_ref=dref.at[dat], send_sem=send_sem.at[u["index"]], recv_sem=recv_sem.at[u["index"]],
            device_id=peers[u["to"]], device_id_type=MESH_ID,
        )

    copies = {name: copy(name) for name in plan.units}
    arrived, opened = set(), False
    for name in order:
        step = plan.steps[name]
        for u in step["recv"]:
            if u not in arrived:
                copies[u].wait_recv()
                arrived.add(u)
        if step["fn"] is not None:
            step["fn"]()
        if step["send"] and not opened:
            pl.semaphore_wait(barrier, len(greeted))
            opened = True
        for u in step["send"]:
            copies[u].start()
    for name in plan.units:
        if name not in arrived:
            copies[name].wait_recv()
        copies[name].wait_send()


def scratch_shapes(rows, size, deep, count):
    bf, fp, v = jnp.bfloat16, jnp.float32, pltpu.VMEM
    blocks, where, seg = need_order()
    shapes = [
        v((4 * rows, size), bf), v((deep + 1, rows, rows), bf), v((NY * NC * size, size), bf), v((len(blocks), rows, size), fp),
        v((len(STREAMS), NY, NC, rows, size), bf), v((len(STREAMS) * NX * NZ, rows, size), bf),
        v((4, NY, NC, rows, size), bf), v((4 * rows, size), bf),
        pltpu.SemaphoreType.DMA((count,)), pltpu.SemaphoreType.DMA((count,)), pltpu.SemaphoreType.DMA((6 + NY,)),
    ]
    for kind in STREAMS:
        n1, n2 = sizes(kind)
        first, second = v((2, max(n1 // 2, 1), n2, rows, size), bf), v((2, max(n2 // 2, 1), rows, size), bf)
        if {"z": "x", "x": "z"}[kind] in DIRECT["B"]:
            second = v((max(n2 - 1, 1), rows, size), bf)
        shapes += [first, first, second, second, v((n2, rows, size), fp)]
    return shapes


def local(features, tiles, tile_slot, tile_col, tile_id, touched, weight, readers):
    edge = lax.axis_index("edge")
    block = tiles.shape[1]
    size = features.shape[1]
    deep = tiles.shape[0]
    blocks, where, seg = need_order()
    group = 4 if all((hi - lo) % 4 == 0 for _, lo, hi in seg) else 1
    seq = jnp.array([rx * 1024 + rz * 4 + j for rx, rz, j in blocks], jnp.int32)
    lists = lax.dynamic_index_in_dim(touched, edge, 0, keepdims=False).reshape(-1)
    keys = jnp.arange(lists.shape[0] * 4, dtype=jnp.int32)
    pair = tile_slot * 4 + tile_col
    table = deep + jnp.sum(jnp.where(keys[:, None] == pair[None, :], tile_id[None, :] - deep, 0), axis=1)
    args = (table.astype(jnp.int32), lists, readers, seq, features, tiles, weight)
    plan, order = kernel(True, group, None, *args, None, None, *([None] * 31))
    used = sorted({u["to"] for u in plan.units.values()} | {(u["to"][0], -u["to"][1] % {"x": NX, "z": NZ, "y": NY, "core": NC}[u["to"][0]]) for u in plan.units.values()})
    vmem = pl.BlockSpec(memory_space=pltpu.VMEM)
    smem = pl.BlockSpec(memory_space=pltpu.SMEM)
    hbm = pl.BlockSpec(memory_space=pltpu.HBM)
    return pl.pallas_call(
        functools.partial(kernel, False, group, used),
        out_shape=(
            jax.ShapeDtypeStruct(features.shape, jnp.bfloat16),
            jax.ShapeDtypeStruct((readers.shape[0] * block, size), jnp.bfloat16),
        ),
        in_specs=[smem, smem, smem, smem, hbm, hbm, hbm],
        out_specs=(vmem, vmem),
        scratch_shapes=scratch_shapes(block, size, deep, len(plan.units)),
        compiler_params=pltpu.CompilerParams(collective_id=0, has_side_effects=True, vmem_limit_bytes=52 << 20),
        name="layer",
    )(*args)


def solution(mesh):
    in_specs = (
        P("edge", "feat"),
        P("edge", None, None),
        P("edge"),
        P("edge"),
        P("edge"),
        P(),
        P(None, "feat"),
        P("edge"),
    )
    out_specs = (P("edge", "feat"), P("edge", "feat"))
    return jax.shard_map(local, mesh=mesh, in_specs=in_specs, out_specs=out_specs, check_vma=False)
```
